32 devices in a mesh: group: 2 (over y), seq: 4 (over z), exp: 2 (over x), tp: 2 (over core).
Axes of the slice: x: 2, y: 2, z: 4, core: 2. Of those that a mesh axis runs over, the one named last changes fastest.
Arguments:
- queries: bfloat16 [4, 512, 4096], P(('group', 'exp'), ('seq', 'tp')), parts along dimension 0, may hold values from -18 to 18
- keys_values: bfloat16 [4, 768, 2, 1024], P(('group', 'exp'), ('seq', 'tp')), parts along dimension 0, may hold values from -18 to 18
- prompt_lengths: int32 [4], P(('group', 'exp')), parts along dimension 0, may hold values from 1 to 256, 384 in all
- routes: int32 [4, 512, 8], P(('group', 'exp'), ('seq', 'tp')), parts along dimension 0, may hold values from 0 to 63, all different within a row; in each aligned block of 64 rows (0 to 63, 64 to 127, ..., all dimensions but the last counted through in order) at most 16 rows name the same one
- gate_weights: float32 [4, 512, 8], P(('group', 'exp'), ('seq', 'tp')), parts along dimension 0, may hold values from 0.05 to 0.5
- norm_gain: float32 [4096], replicated, may hold values from 0.5 to 1.5
- w_gate: bfloat16 [2, 4096, 2048], P('tp', None, 'seq'), may hold values from -0.09375 to 0.09375
- w_up: bfloat16 [2, 4096, 2048], P('tp', None, 'seq'), may hold values from -0.09375 to 0.09375
- w_down: bfloat16 [2, 2048, 4096], P('tp', 'seq'), may hold values from -0.125 to 0.125
Outputs:
- mixed: bfloat16 [4, 512, 4096], P(('group', 'exp'), ('seq', 'tp')), parts along dimension 0
The draws below stay inside these ranges and needn't reach their ends.
There are 2 independent parts, one for each index of `group`. The reference program is written for one: setup_inputs(seed, part) draws one part's arguments, and reference() takes and returns one part's arrays. A program takes and returns all parts, laid end to end along the dimension named above; an argument that names none is the same for every part. Nothing has to cross between parts.
Inputs may be any that keep to these rules, and one draw needn't show every extreme that they name: Each token's 8 routes name different experts. Among the 64 consecutive tokens of one device no expert is named by more than 16 tokens, a bound that some block reaches.
All inputs are finite; a program needn't handle non-finite values. No bound on the sum of `prompt_lengths` on one device may be relied on, other than what follows from the above.
Results may differ from the reference program's by a relative error of at most 0.02.
Values may be sent and summed in bfloat16 or wider, within the bound.
A program may use at most 128 MiB of HBM per device.

```python
import math
import jax
import jax.numpy as jnp
import numpy as np
from jax import lax

D = 4096
HEADS = 32
KV_HEADS = 8
HEAD_DIM = 128
EXPERTS = 64
TOP = 8
FF = 2048
PROMPT = 256
TOK_DEV = 64
IMAGES = 2
LEN = 512
KEYS = 768
WIN = 2
CAP = 16
N_SEQ = 4


def attention_pair(key):
    base_key = jax.random.fold_in(key, 7001)
    pair_width = KV_HEADS * HEAD_DIM
    pair_rows = jnp.clip(jax.random.normal(jax.random.fold_in(base_key, 1), (IMAGES, KEYS, 2, pair_width), jnp.float32), -3.0, 3.0)
    column_scale = jnp.exp(jax.random.uniform(jax.random.fold_in(base_key, 2), (pair_width,), jnp.float32, 0.0, math.log(10.0))) / 3.0
    query_rows = jnp.clip(jax.random.normal(jax.random.fold_in(base_key, 3), (IMAGES, LEN, HEADS * HEAD_DIM), jnp.float32), -3.0, 3.0)
    pair_rows = pair_rows.at[:, :, 1, :].multiply(column_scale)
    return (query_rows, pair_rows)


def draw_queries(key, part):
    return attention_pair(key)[0].astype(jnp.bfloat16)


def draw_keys_values(key, part):
    return attention_pair(key)[1].astype(jnp.bfloat16)


def levels(rng, extent, split, smallest, top_value):
    def one(dim, shards_of):
        steps = jax.random.uniform(jax.random.fold_in(jax.random.fold_in(rng, 6), dim), (shards_of,), jnp.float32, smallest / len(split), top_value / len(split))
        return jnp.repeat(jnp.exp(steps), extent[dim] // shards_of).reshape((-1,) + (1,) * (len(extent) - dim - 1))

    loudness = one(*split[0])
    for cut in split[1:]:
        loudness = loudness * one(*cut)
    return loudness


def split_up(amount, total, limit, lean):
    loads = [(1 << 20) // math.isqrt(grade ** lean) + 1 for grade in range(2, amount + 1)]
    rest, counts = total - limit - (amount - 1), [1] * (amount - 1)
    while rest > 0:
        free = [i for i in range(amount - 1) if counts[i] < limit]
        whole, budget = sum([loads[i] for i in free]), rest
        for i in free:
            addition = min(limit - counts[i], max(1, budget * loads[i] // whole), rest)
            counts[i] = counts[i] + addition
            rest = rest - addition
    return np.array([limit] + counts)


def ragged(key, number_of, total, reach, slope):
    if number_of == 2:
        one = jax.random.randint(key, (), max(1, total - reach), min(reach, total - 1) + 1)
        return jnp.stack([one, total - one])
    lengths = jnp.asarray(split_up(number_of, total, reach, slope), jnp.int32)
    couples = (number_of - 1) // 2
    donor, receiver = lengths[1:1 + 2 * couples:2], lengths[2:2 + 2 * couples:2]
    slack = jnp.minimum(donor - 1, reach - receiver)
    shifted = jax.random.randint(jax.random.fold_in(key, 1), (couples,), 0, 1 << 20) % (slack + 1)
    lengths = lengths.at[1:1 + 2 * couples:2].set(donor - shifted).at[2:2 + 2 * couples:2].set(receiver + shifted)
    return lengths[jax.random.permutation(jax.random.fold_in(key, 2), number_of)]


def assign_block(own_key, own, number, rows, number_of, top, limit, skew):
    ranking = jax.random.permutation(own_key, number_of)
    crowded, ordinary = portions_of(number_of, rows * top, limit, skew, True), portions_of(number_of, rows * top, limit, skew, False)
    places = jnp.arange(number_of)

    def named(tallies, rotation):
        used = int((tallies > 0).sum())
        fixed = max(1, used // 4)
        passed = fixed + (places - fixed + rotation * (used - fixed)) % max(1, number_of - fixed)
        return jnp.zeros((number_of,), jnp.int32).at[ranking[jnp.where(places < fixed, places, passed)]].set(jnp.asarray(tallies, jnp.int32))

    tallies = jnp.where(number % 4 == 0, named(crowded, number // 4), named(ordinary, number - number // 4 - 1))
    mixed = jax.random.permutation(jax.random.fold_in(own, 3), number_of)
    source_of, receiver = mixed[0:number_of // 2 * 2:2], mixed[1:number_of // 2 * 2:2]
    room = jnp.minimum(tallies[source_of] - 1, limit - tallies[receiver]) // 2
    room = jnp.where((source_of == ranking[0]) | (receiver == ranking[0]) | (tallies[receiver] == 0), 0, jnp.maximum(room, 0))
    passed = jax.random.randint(jax.random.fold_in(own, 4), (number_of // 2,), 0, 1 << 20) % (room + 1)
    tallies = tallies.at[source_of].add(-passed).at[receiver].add(passed)
    labels = jnp.searchsorted(jnp.cumsum(tallies), jnp.arange(rows * top), side="right").astype(jnp.int32)
    listing = labels.reshape(top, rows).T
    listing = listing[jax.random.permutation(jax.random.fold_in(own, 1), rows)]
    rotation = jax.random.randint(jax.random.fold_in(own, 2), (rows, 1), 0, top)
    return jnp.take_along_axis(listing, (jnp.arange(top)[None, :] + rotation) % top, axis=1)


def portions_of(amount, total, limit, slope, full):
    loads = [(1 << 20) // math.isqrt(grade ** slope) + 1 for grade in range(1, amount + 1)]
    largest = limit if full else min(limit, max(-(-total // amount), total * loads[0] // sum(loads)))
    least = 1 if total - largest >= amount - 1 else 0
    given, rest = [largest] + [least] * (amount - 1), total - largest - least * (amount - 1)
    while rest > 0:
        candidates = [i for i in range(1, amount) if given[i] < largest] or [i for i in range(1, amount) if given[i] < limit]
        mass, budget = sum([loads[i] for i in candidates]), rest
        for i in candidates:
            addition = min(limit - given[i], max(1, budget * loads[i] // mass), rest)
            given[i] = given[i] + addition
            rest = rest - addition
    return np.array(given)


def scatter_about(stream_key, shape, spread, limit, shards=(), dtype=jnp.bfloat16):
    values = jax.random.normal(stream_key, shape, jnp.float32) * spread
    if len(shards) > 0:
        values = levels(stream_key, shape, shards, -0.22, 0.18) * values
    return jnp.clip(values, min=-limit, max=limit).astype(dtype)


def setup_inputs(seed: int = 0, part: int = 0) -> dict:
    streams_of = jax.random.split(jax.random.key(seed), 10)
    own_keys = jax.random.split(jax.random.fold_in(streams_of[9], part), 10)
    queries = draw_queries(jax.random.fold_in(jax.random.fold_in(streams_of[9], part), 71), part)
    keys_values = draw_keys_values(jax.random.fold_in(jax.random.fold_in(streams_of[9], part), 71), part)
    prompt_lengths = ragged(own_keys[2], IMAGES, (IMAGES + 1) * PROMPT // 2, PROMPT, 0).astype(jnp.int32)
    routes_keys = jax.random.split(jax.random.fold_in(own_keys[3], 1), IMAGES * LEN // TOK_DEV)
    routes_turns = jax.random.permutation(jax.random.fold_in(own_keys[3], 3), IMAGES * LEN // TOK_DEV)
    routes = jax.vmap(lambda own, number: assign_block(jax.random.fold_in(own_keys[3], 2), own, number, TOK_DEV, EXPERTS, TOP, CAP, 2))(routes_keys, routes_turns).reshape((IMAGES, LEN, TOP))
    gate_weights = jnp.clip(jnp.exp(math.log(0.5) - 2.3025851 * jax.random.uniform(own_keys[4], (IMAGES, LEN, TOP), jnp.float32) ** levels(own_keys[4], (IMAGES, LEN, TOP), ((0, 2), (1, 8)), -0.2, 0.2)), 0.05, 0.5)
    norm_gain = jnp.clip(1.0 + 0.1 * jax.random.normal(streams_of[5], (D,), jnp.float32), 0.5, 1.5)
    w_gate = scatter_about(streams_of[6], (WIN, D, FF), D ** -0.5, 0.09375, ((0, 2), (2, 4)))
    w_up = scatter_about(streams_of[7], (WIN, D, FF), D ** -0.5, 0.09375, ((0, 2), (2, 4)))
    w_down = scatter_about(streams_of[8], (WIN, FF, D), FF ** -0.5, 0.125, ((0, 2), (1, 4)))
    return dict(queries=queries, keys_values=keys_values, prompt_lengths=prompt_lengths, routes=routes, gate_weights=gate_weights, norm_gain=norm_gain, w_gate=w_gate, w_up=w_up, w_down=w_down)


epsilon = 1e-06
masked_score = -1e+30

def rounded(values):
    return lax.optimization_barrier(values.astype(jnp.bfloat16)).astype(jnp.float32)

def attend_image(operands):
    queries_image, pairs_image, prompt_length = operands
    group = HEADS // KV_HEADS
    query_f = jnp.transpose(queries_image.astype(jnp.float32).reshape(LEN, KV_HEADS, group, HEAD_DIM), (1, 0, 2, 3))
    key_f = jnp.transpose(pairs_image[:, 0].astype(jnp.float32).reshape(KEYS, KV_HEADS, HEAD_DIM), (1, 0, 2))
    value_f = jnp.transpose(pairs_image[:, 1].astype(jnp.float32).reshape(KEYS, KV_HEADS, HEAD_DIM), (1, 0, 2))
    position = jnp.arange(KEYS).astype(jnp.int32)
    allowed = (position >= PROMPT) | (position < prompt_length)

    def one_head(pieces):
        query_head, key_head, value_head = pieces
        scores = jnp.einsum('lrd,kd->rlk', query_head, key_head) * (1.0 / math.sqrt(HEAD_DIM))
        scores = jnp.where(allowed, scores, masked_score)
        largest = lax.optimization_barrier(jnp.max(scores, axis=-1, keepdims=True))
        weights = jnp.where(allowed, jnp.exp(scores - largest), 0.0)
        totals = lax.optimization_barrier(jnp.sum(weights, axis=-1))
        summed = jnp.einsum('rlk,kd->lrd', rounded(weights), value_head)
        return summed / jnp.transpose(totals)[..., None]
    result = lax.map(one_head, (query_f, key_f, value_f))
    return jnp.transpose(result, (1, 0, 2, 3)).reshape(LEN, D).astype(jnp.bfloat16)

def reference(queries, keys_values, prompt_lengths, routes, gate_weights, norm_gain, w_gate, w_up, w_down):
    attended = lax.map(attend_image, (queries, keys_values, prompt_lengths))
    token_count = IMAGES * LEN
    flat_attended = attended.reshape(token_count, D).astype(jnp.float32)
    mean_square = lax.optimization_barrier(jnp.mean(flat_attended * flat_attended, axis=-1, keepdims=True))
    normed = (flat_attended * lax.rsqrt(mean_square + epsilon) * norm_gain).astype(jnp.bfloat16)
    route_ids = routes.reshape(token_count, TOP)
    route_gates = gate_weights.reshape(token_count, TOP)
    most_rows = token_count // TOK_DEV * CAP
    block_width = FF // N_SEQ
    combined = jnp.zeros((token_count, D), jnp.float32)
    for expert in range(WIN):
        hits = route_ids == expert
        member = jnp.any(hits, axis=1)
        weight = lax.optimization_barrier(jnp.sum(jnp.where(hits, route_gates, 0.0), axis=1))
        positions = jnp.nonzero(member, size=most_rows, fill_value=0)[0].astype(jnp.int32)
        filled = jnp.arange(most_rows) < jnp.sum(member.astype(jnp.int32))
        rows = normed[positions]
        gate_part = jnp.dot(rows, w_gate[expert], preferred_element_type=jnp.float32)
        up_part = jnp.dot(rows, w_up[expert], preferred_element_type=jnp.float32)
        hidden_units = (jax.nn.silu(gate_part) * up_part).astype(jnp.bfloat16)
        hidden_blocks = hidden_units.astype(jnp.float32).reshape(most_rows, N_SEQ, block_width)
        down_blocks = w_down[expert].astype(jnp.float32).reshape(N_SEQ, block_width, D)
        block_sums = rounded(jnp.einsum('rbf,bfd->rbd', hidden_blocks, down_blocks))
        expert_out = rounded(lax.optimization_barrier(jnp.sum(block_sums, axis=1)))
        scale_rows = jnp.where(filled, weight[positions], 0.0)
        combined = combined.at[positions].add(scale_rows[:, None] * expert_out)
    mixed = (flat_attended + combined).astype(jnp.bfloat16)
    return mixed.reshape(IMAGES, LEN, D)
```

```python
import functools
import math

import jax
import jax.numpy as jnp
from jax import lax
from jax.experimental import pallas as pl
from jax.experimental.pallas import tpu as pltpu
from jax.sharding import PartitionSpec as P

HEADS = 32
KV_HEADS = 8
HEAD_DIM = 128
PROMPT = 256
CAP = 16
LEAD = 2
SUM_CHUNKS = 4
ROW_CHUNKS = 4
ROW_LAG = 2
GUEST_LAG = 1
HOLD = 7
KV_LAG = 2
SIB_LAG = 1
END_LEAD = 4
SUM_LAG = 3

epsilon = 1e-06
masked_score = -1e30
MESH = pl.DeviceIdType.MESH
F32 = jnp.float32
BF16 = jnp.bfloat16


def kernel(
    n, plen_ref, kv_hbm, routes_hbm, gates_hbm, gain_hbm, q_hbm, wg_hbm, wu_hbm, wd_hbm,
    out_ref,
    routes_ref, gates_ref, gain_ref, qbuf, wg, wu, wd, kvbuf, att, groutes, sel, xsel, xbuf, part, rbuf, fin, ret, acc,
    w_sem, kv_local, kv_send, kv_recv, q_send, q_recv, g_sem, x_send, xs_send, f_send, x_recv,
    a_sem, r_send, r_recv, y_send, y_recv,
):
    z = lax.axis_index("seq")
    c = lax.axis_index("tp")
    sib = 1 - c
    has_left = z > 0
    has_right = z < n - 1
    end = (z == 0) | (z == n - 1)
    inner = (z > 0) & (z < n - 1)
    hosts = (z == 1) | (z == n - 2)
    guest = jnp.where(z == 1, 0, n - 1)
    host = jnp.where(z == 0, 1, n - 2)
    go_left = z > 1
    go_right = z < n - 2
    left, right, other = {"seq": z - 1}, {"seq": z + 1}, {"tp": sib}
    tokens = qbuf.shape[1]
    piece = kv_hbm.shape[2]
    groups = HEADS // KV_HEADS
    span = groups * HEAD_DIM
    width = att.shape[2]
    two = 2
    lag = KV_LAG * (n - 3) + SIB_LAG

    barrier = pltpu.get_barrier_semaphore()

    @pl.when(has_left)
    def _():
        for e in range(two):
            pl.semaphore_signal(barrier, inc=1, device_id={"seq": z - 1, "tp": e}, device_id_type=MESH)

    @pl.when(has_right)
    def _():
        for e in range(two):
            pl.semaphore_signal(barrier, inc=1, device_id={"seq": z + 1, "tp": e}, device_id_type=MESH)

    pl.semaphore_signal(barrier, inc=1, device_id=other, device_id_type=MESH)

    loads = [
        pltpu.make_async_copy(q_hbm, qbuf.at[0], w_sem.at[0]),
        pltpu.make_async_copy(wg_hbm, wg, w_sem.at[1]),
        pltpu.make_async_copy(wu_hbm, wu, w_sem.at[2]),
        pltpu.make_async_copy(wd_hbm, wd, w_sem.at[3]),
    ]
    own_kv = [
        pltpu.make_async_copy(kv_hbm.at[h], kvbuf.at[h, :, z, c], kv_local.at[h])
        for h in range(KV_HEADS)
    ]
    small = [
        pltpu.make_async_copy(routes_hbm, routes_ref, w_sem.at[4]),
        pltpu.make_async_copy(gates_hbm, gates_ref, w_sem.at[5]),
        pltpu.make_async_copy(gain_hbm, gain_ref, w_sem.at[6]),
    ]
    for copy in own_kv + small:
        copy.start()
    loads[0].start()

    for copy in own_kv + small:
        copy.wait()
    loads[0].wait()

    tri = (
        lax.broadcasted_iota(jnp.int32, (tokens, tokens), 0)
        <= lax.broadcasted_iota(jnp.int32, (tokens, tokens), 1)
    ).astype(F32)
    slots = lax.broadcasted_iota(jnp.int32, (CAP, tokens), 0).astype(F32)

    def picks(routes):
        chosen = []
        for e in range(two):
            hit = jnp.max((routes == e).astype(F32), axis=0, keepdims=True)
            rank = jnp.dot(jnp.broadcast_to(hit, (CAP, tokens)), tri, preferred_element_type=F32)
            chosen.append(jnp.where((rank - 1.0 == slots) & (hit > 0.0), 1.0, 0.0))
        return jnp.concatenate(chosen, axis=0)

    sel[0] = picks(routes_ref[...]).astype(BF16)

    pl.semaphore_wait(barrier, 1 + 2 * has_left.astype(jnp.int32) + 2 * has_right.astype(jnp.int32))

    def remote(src, dst, send, recv, device):
        return pltpu.make_async_remote_copy(
            src_ref=src, dst_ref=dst, send_sem=send, recv_sem=recv,
            device_id=device, device_id_type=MESH,
        )

    def kv_copy(h, oz, oc, way, device):
        slot = kvbuf.at[h, :, oz, oc]
        return remote(slot, slot, kv_send.at[h, oz, way], kv_recv.at[h, oz, oc], device)

    def pass_kv(h, oz, way):
        if way != 1:
            @pl.when(go_left)
            def _():
                kv_copy(h, oz, c, 0, left).start()

        if way != 0:
            @pl.when(go_right)
            def _():
                kv_copy(h, oz, c, 1, right).start()

        @pl.when(inner)
        def _():
            kv_copy(h, oz, c, 2, other).start()

    def query_copy(h):
        cols = pl.ds(pl.multiple_of(h * span, span), span)
        return remote(
            qbuf.at[0, :, cols], qbuf.at[1, :, cols], q_send.at[h], q_recv.at[h], {"seq": host}
        )

    def route_copy():
        return remote(routes_ref, groutes, g_sem.at[0], g_sem.at[1], {"seq": host})

    @pl.when(end)
    def _():
        route_copy().start()

    @pl.when(inner)
    def _():
        for h in range(LEAD):
            pass_kv(h, z, 2)

    @pl.when(end)
    def _():
        for h in range(END_LEAD):
            pass_kv(h, z, 2)
        for h in range(KV_HEADS):
            query_copy(h).start()
            if h + END_LEAD < KV_HEADS:
                pass_kv(h + END_LEAD, z, 2)

    for load in loads[1:]:
        load.start()

    @pl.when(hosts)
    def _():
        route_copy().wait_recv()
        sel[1] = picks(groutes[...]).astype(BF16)

    plen = plen_ref[0]
    keys = n * two * piece
    position = lax.broadcasted_iota(jnp.int32, (1, keys), 1)
    allowed = (position >= PROMPT) | (position < plen)

    def attend(h, s):
        base = pl.multiple_of(h * span, span)
        query = jnp.concatenate(
            [qbuf[s, :, pl.ds(base + g * HEAD_DIM, HEAD_DIM)] for g in range(groups)], axis=0
        )
        key_rows = kvbuf[h, 0].reshape(keys, HEAD_DIM)
        value_rows = kvbuf[h, 1].reshape(keys, HEAD_DIM)
        scores = lax.dot_general(
            query, key_rows, (((1,), (1,)), ((), ())), preferred_element_type=F32
        ) * (1.0 / math.sqrt(HEAD_DIM))
        scores = jnp.where(allowed, scores, masked_score)
        weights = jnp.exp(scores - jnp.max(scores, axis=1, keepdims=True))
        total = jnp.sum(weights, axis=1, keepdims=True)
        summed = jnp.dot(weights.astype(BF16), value_rows, preferred_element_type=F32)
        result = (summed / total).astype(BF16)
        for g in range(groups):
            att[s, :, pl.ds(base + g * HEAD_DIM, HEAD_DIM)] = result[g * tokens:(g + 1) * tokens]

    cut = width // ROW_CHUNKS
    per_cut = KV_HEADS // ROW_CHUNKS

    def columns(k):
        return pl.ds(pl.multiple_of(k * cut, cut), cut)

    def origin_of(s):
        return jnp.where(s == 0, z, guest)

    def row_copy(s, e, k, way):
        return remote(
            xsel.at[s, e, :, columns(k)], xbuf.at[origin_of(s), c, :, columns(k)],
            x_send.at[s, e, k, way], x_recv.at[origin_of(s), c, k],
            {"seq": z - 1 if way == 0 else z + 1, "tp": e},
        )

    def near_copy(s, k):
        return remote(
            xsel.at[s, sib, :, columns(k)], xbuf.at[origin_of(s), c, :, columns(k)],
            xs_send.at[s, k], x_recv.at[origin_of(s), c, k], other,
        )

    def far_copy(oz, oc, k, way):
        slot = xbuf.at[oz, oc, :, columns(k)]
        return remote(
            slot, slot, f_send.at[oz, oc, k], x_recv.at[oz, oc, k], left if way == 0 else right
        )

    def whole_rows(s, k):
        return k * per_cut + per_cut - 1 + lag + s * GUEST_LAG

    def start_rows(s, k, late):
        for way, edge in ((0, z == 1), (1, z == n - 2)):
            @pl.when(~edge if late else edge)
            def _():
                for e in range(two):
                    row_copy(s, e, k, way).start()

    def send_rows(r, s, k):
        picked = jnp.dot(sel[s], att[s, :, columns(k)], preferred_element_type=F32).astype(BF16)
        for e in range(two):
            xsel[s, e, :, columns(k)] = picked[e * CAP:(e + 1) * CAP]
        @pl.when((s == 1) & (r >= HOLD))
        def _():
            start_rows(s, k, True)

        start_rows(s, k, False)
        near_copy(s, k).start()
        xbuf[origin_of(s), c, :, columns(k)] = xsel[s, c, :, columns(k)]

    def relay(oz, k, ok, way):
        @pl.when(ok)
        def _():
            for oc in range(two):
                far_copy(oz, oc, k, way).wait_recv()
                far_copy(oz, oc, k, way).start()

    def relay_round(r):
        def one(k, inner_carry):
            for d in range(1, n - 2):
                due = r == jnp.maximum(whole_rows(1, k), HOLD) + ROW_LAG * d
                relay(0, k, due & (z - d == 1), 1)
                relay(n - 1, k, due & (z + d == n - 2), 0)
            return inner_carry

        lax.fori_loop(0, ROW_CHUNKS, one, 0)

    def kv_round(r, carry):
        @pl.when(r + LEAD < KV_HEADS)
        def _():
            pass_kv(r + LEAD, z, 2)

        for d in range(1, n - 1):
            h = r - KV_LAG * (d - 1)
            live = (h >= 0) & (h < KV_HEADS)

            @pl.when(live & (z - d >= 0))
            def _():
                kv_copy(h, z - d, c, 2, other).wait_recv()
                pass_kv(h, z - d, 1)

            @pl.when(live & (z + d < n))
            def _():
                kv_copy(h, z + d, c, 2, other).wait_recv()
                pass_kv(h, z + d, 0)

        @pl.when(r == HOLD)
        def _():
            for k in range(ROW_CHUNKS):
                if whole_rows(1, k) < HOLD:
                    @pl.when(hosts)
                    def _():
                        start_rows(1, k, True)

        def one(s, inner_carry):
            h = r - lag - s * GUEST_LAG

            @pl.when((h >= 0) & (h < KV_HEADS) & ((s == 0) | hosts))
            def _():
                @pl.when(s == 0)
                def _():
                    for oz in range(n):
                        kv_copy(h, oz, sib, 2, other).wait_recv()

                @pl.when(s == 1)
                def _():
                    query_copy(h).wait_recv()

                attend(h, s)

                @pl.when(h % per_cut == per_cut - 1)
                def _():
                    send_rows(r, s, h // per_cut)

            return inner_carry

        lax.fori_loop(0, two, one, 0)
        relay_round(r)
        return carry

    attend_rounds = max(KV_HEADS + lag + GUEST_LAG, HOLD + 1)
    relay_rounds = attend_rounds + ROW_LAG * (n - 3)

    @pl.when(inner)
    def _():
        lax.fori_loop(0, attend_rounds, kv_round, 0)

        def own_rows(k, carry):
            start_rows(0, k, True)
            return carry

        lax.fori_loop(0, ROW_CHUNKS, own_rows, 0)

    for load in loads[1:]:
        load.wait()

    rows_here = two * CAP
    strip = width // SUM_CHUNKS
    pairs = n // two

    def expert(first, count):
        rows = xbuf[pl.ds(first, count)].reshape(count * rows_here, width).astype(F32)
        mean_square = jnp.mean(rows * rows, axis=1, keepdims=True)
        normed = (rows * lax.rsqrt(mean_square + epsilon) * gain_ref[...]).astype(BF16)
        gate_part = jnp.dot(normed, wg[...], preferred_element_type=F32)
        up_part = jnp.dot(normed, wu[...], preferred_element_type=F32)
        hidden = (gate_part / (1.0 + jnp.exp(-gate_part)) * up_part).astype(BF16)
        for k in range(SUM_CHUNKS):
            done = jnp.dot(
                hidden, wd[:, k * strip:(k + 1) * strip], preferred_element_type=F32
            ).astype(BF16)
            for i in range(count):
                part[first + i, k] = done[i * rows_here:(i + 1) * rows_here]

    def sum_copy(way, dest, k, device):
        return remote(
            part.at[dest, k], rbuf.at[way, dest, k], r_send.at[way, dest, k], r_recv.at[way, dest, k],
            device,
        )

    def att_copy():
        return remote(att.at[1], att.at[0], a_sem.at[0], a_sem.at[1], {"seq": guest})

    def gather_rows(oz):
        @pl.when(end)
        def _():
            for oc in range(two):
                for k in range(ROW_CHUNKS):
                    far_copy(oz, oc, k, 0).wait_recv()

        @pl.when(inner & ((oz == z) | (hosts & (oz == guest))))
        def _():
            for k in range(ROW_CHUNKS):
                far_copy(oz, sib, k, 0).wait_recv()

    def send_sums(dest):
        @pl.when((z == 0) & (dest > 0))
        def _():
            for k in range(SUM_CHUNKS):
                sum_copy(0, dest, k, right).start()

        @pl.when((z == n - 1) & (dest < n - 1))
        def _():
            for k in range(SUM_CHUNKS):
                sum_copy(1, dest, k, left).start()

    near = z // two

    @pl.when(hosts | end)
    def _():
        for i in range(two):
            gather_rows(near * two + i)
        expert(near * two, two)
        for i in range(two):
            send_sums(near * two + i)

    @pl.when(inner)
    def _():
        def later(r, carry):
            relay_round(r)
            return carry

        lax.fori_loop(attend_rounds, relay_rounds, later, 0)
        for d in range(1, n - 2):
            def own_relay(k, carry):
                relay(z - d, k, z - d >= 1, 1)
                relay(z + d, k, z + d <= n - 2, 0)
                return carry

            lax.fori_loop(0, ROW_CHUNKS, own_relay, 0)

    @pl.when(hosts)
    def _():
        att_copy().start()

    def far_step(j, carry):
        p = lax.rem(near + j // two, pairs)
        i = j % two
        oz = p * two + jnp.where(p == pairs - 1, 1 - i, i)

        @pl.when((j >= two) | ~(hosts | end))
        def _():
            gather_rows(oz)
            expert(oz, 1)
            send_sums(oz)

        return carry

    lax.fori_loop(0, n, far_step, 0)

    def pass_sum(way, dest, k, joins, device):
        @pl.when(joins)
        def _():
            sum_copy(way, dest, k, device).wait_recv()
            part[dest, k] = (part[dest, k].astype(F32) + rbuf[way, dest, k].astype(F32)).astype(BF16)

        sum_copy(way, dest, k, device).start()

    def sum_round(t, carry):
        i = t - SUM_LAG * z
        dest = n - 1 - i // SUM_CHUNKS

        @pl.when(inner & (i >= 0) & (dest > z))
        def _():
            pass_sum(0, dest, i % SUM_CHUNKS, has_left, right)

        i_back = t - SUM_LAG * (n - 1 - z)
        home = i_back // SUM_CHUNKS

        @pl.when(inner & (i_back >= 0) & (home < z))
        def _():
            pass_sum(1, home, i_back % SUM_CHUNKS, has_right, left)

        return carry

    lax.fori_loop(0, (SUM_CHUNKS + SUM_LAG) * (n - 1), sum_round, 0)

    def result_copy(oc, k):
        cols = pl.ds(k * strip, strip)
        return remote(fin.at[sib, :, cols], ret.at[oc, :, cols], y_send.at[k], y_recv.at[k], other)

    for k in range(SUM_CHUNKS):
        cols = slice(k * strip, (k + 1) * strip)
        acc[...] = part[z, k].astype(F32)

        @pl.when(has_left)
        def _():
            sum_copy(0, z, k, right).wait_recv()
            acc[...] += rbuf[0, z, k].astype(F32)

        @pl.when(has_right)
        def _():
            sum_copy(1, z, k, left).wait_recv()
            acc[...] += rbuf[1, z, k].astype(F32)

        fin[:, :, cols] = acc[...].astype(BF16).reshape(two, CAP, strip)
        result_copy(c, k).start()
        ret[c, :, cols] = fin[c, :, cols]

    @pl.when(end)
    def _():
        att_copy().wait_recv()

    routes = routes_ref[...]
    gates = gates_ref[...]
    select = picks(routes)
    combine = []
    for e in range(two):
        gate = jnp.sum(jnp.where(routes == e, gates, 0.0), axis=0, keepdims=True)
        combine.append(select[e * CAP:(e + 1) * CAP] * gate)
    cw = jnp.transpose(jnp.concatenate(combine, axis=0))
    first = cw.astype(BF16)
    rest = cw - first.astype(F32)
    second = rest.astype(BF16)
    third = (rest - second.astype(F32)).astype(BF16)
    for k in range(SUM_CHUNKS):
        cols = slice(k * strip, (k + 1) * strip)
        result_copy(sib, k).wait_recv()
        returned = ret[:, :, cols].reshape(rows_here, strip)
        total = (
            jnp.dot(first, returned, preferred_element_type=F32)
            + jnp.dot(second, returned, preferred_element_type=F32)
            + jnp.dot(third, returned, preferred_element_type=F32)
        )
        out_ref[:, cols] = (att[0, :, cols].astype(F32) + total).astype(BF16)

    for k in range(SUM_CHUNKS):
        result_copy(c, k).wait_send()

    def drain_kv(h, carry):
        for oz in range(n):
            @pl.when(go_left & (oz >= z))
            def _():
                kv_copy(h, oz, c, 0, left).wait_send()

            @pl.when(go_right & (oz <= z))
            def _():
                kv_copy(h, oz, c, 1, right).wait_send()

            @pl.when(inner)
            def _():
                kv_copy(h, oz, c, 2, other).wait_send()

        @pl.when(end)
        def _():
            query_copy(h).wait_send()

        return carry

    lax.fori_loop(0, KV_HEADS, drain_kv, 0)

    @pl.when(end)
    def _():
        route_copy().wait_send()

    @pl.when(hosts)
    def _():
        att_copy().wait_send()

    def drain_rows(k, carry):
        for s in range(two):
            @pl.when(inner if s == 0 else hosts)
            def _():
                for e in range(two):
                    for way in range(2):
                        row_copy(s, e, k, way).wait_send()
                near_copy(s, k).wait_send()

        for oz in range(n):
            from_left = (oz < z) & ~((oz == 0) & (z == 1))
            from_right = (oz > z) & ~((oz == n - 1) & (z == n - 2))

            @pl.when(inner & (from_left | from_right))
            def _():
                for oc in range(two):
                    far_copy(oz, oc, k, 0).wait_send()

        return carry

    lax.fori_loop(0, ROW_CHUNKS, drain_rows, 0)

    for oz in range(n):
        for k in range(SUM_CHUNKS):
            @pl.when(oz > z)
            def _():
                sum_copy(0, oz, k, right).wait_send()

            @pl.when(oz < z)
            def _():
                sum_copy(1, oz, k, left).wait_send()


def body(
    queries, keys_values, prompt_lengths, routes, gate_weights, norm_gain, w_gate, w_up, w_down
):
    n = lax.axis_size("seq")
    tokens, width = queries.shape[1:]
    piece = keys_values.shape[1]
    ff = w_gate.shape[2]
    kv = keys_values[0].reshape(piece, 2, KV_HEADS, HEAD_DIM).transpose(2, 1, 0, 3)
    top = routes.shape[2]
    strip = width // SUM_CHUNKS
    vmem = pl.BlockSpec(memory_space=pltpu.VMEM)
    hbm = pl.BlockSpec(memory_space=pltpu.HBM)
    dma = pltpu.SemaphoreType.DMA
    mixed = pl.pallas_call(
        functools.partial(kernel, n),
        out_shape=jax.ShapeDtypeStruct((tokens, width), BF16),
        in_specs=[pl.BlockSpec(memory_space=pltpu.SMEM)] + [hbm] * 8,
        out_specs=vmem,
        scratch_shapes=[
            pltpu.VMEM((top, tokens), jnp.int32),
            pltpu.VMEM((top, tokens), F32),
            pltpu.VMEM((1, width), F32),
            pltpu.VMEM((2, tokens, width), BF16),
            pltpu.VMEM((width, ff), BF16),
            pltpu.VMEM((width, ff), BF16),
            pltpu.VMEM((ff, width), BF16),
            pltpu.VMEM((KV_HEADS, 2, n, 2, piece, HEAD_DIM), BF16),
            pltpu.VMEM((2, tokens, width), BF16),
            pltpu.VMEM((top, tokens), jnp.int32),
            pltpu.VMEM((2, 2 * CAP, tokens), BF16),
            pltpu.VMEM((2, 2, CAP, width), BF16),
            pltpu.VMEM((n, 2, CAP, width), BF16),
            pltpu.VMEM((n, SUM_CHUNKS, 2 * CAP, strip), BF16),
            pltpu.VMEM((2, n, SUM_CHUNKS, 2 * CAP, strip), BF16),
            pltpu.VMEM((2, CAP, width), BF16),
            pltpu.VMEM((2, CAP, width), BF16),
            pltpu.VMEM((2 * CAP, strip), F32),
            dma((7,)),
            dma((KV_HEADS,)),
            dma((KV_HEADS, n, 3)),
            dma((KV_HEADS, n, 2)),
            dma((KV_HEADS,)),
            dma((KV_HEADS,)),
            dma((2,)),
            dma((2, 2, ROW_CHUNKS, 2)),
            dma((2, ROW_CHUNKS)),
            dma((n, 2, ROW_CHUNKS)),
            dma((n, 2, ROW_CHUNKS)),
            dma((2,)),
            dma((2, n, SUM_CHUNKS)),
            dma((2, n, SUM_CHUNKS)),
            dma((SUM_CHUNKS,)),
            dma((SUM_CHUNKS,)),
        ],
        compiler_params=pltpu.CompilerParams(
            collective_id=0, has_side_effects=True, vmem_limit_bytes=60 * 1024 * 1024
        ),
    )(
        prompt_lengths, kv, routes[0].T, gate_weights[0].T, norm_gain[None], queries[0],
        w_gate[0], w_up[0], w_down[0],
    )
    return mixed[None]


def solution(mesh):
    return jax.shard_map(
        body,
        mesh=mesh,
        in_specs=(
            P(("group", "exp"), ("seq", "tp"), None),
            P(("group", "exp"), ("seq", "tp"), None, None),
            P(("group", "exp")),
            P(("group", "exp"), ("seq", "tp"), None),
            P(("group", "exp"), ("seq", "tp"), None),
            P(),
            P("tp", None, "seq"),
            P("tp", None, "seq"),
            P("tp", "seq", None),
        ),
        out_specs=P(("group", "exp"), ("seq", "tp"), None),
        check_vma=False,
    )
```

```python
import functools
import math

import jax
import jax.numpy as jnp
from jax import lax
from jax.experimental import pallas as pl
from jax.experimental.pallas import tpu as pltpu
from jax.sharding import PartitionSpec as P

HEADS = 32
KV_HEADS = 8
HEAD_DIM = 128
PROMPT = 256
CAP = 16
LEAD = 2
SUM_CHUNKS = 4
ROW_CHUNKS = 4
ROW_LAG = 2
GUEST_LAG = 1
HOLD = 7
ATT_EARLY = 2
SPLIT = 2
KV_LAG = 2
SIB_LAG = 1
END_LEAD = 4
SUM_LAG = 3

epsilon = 1e-06
masked_score = -1e30
MESH = pl.DeviceIdType.MESH
F32 = jnp.float32
BF16 = jnp.bfloat16


def kernel(
    n, plen_ref, kv_hbm, routes_hbm, gates_hbm, gain_hbm, q_hbm, wg_hbm, wu_hbm, wd_hbm,
    out_ref,
    routes_ref, gates_ref, gain_ref, qbuf, wg, wu, wd, kvbuf, att, groutes, sel, xsel, xbuf, part, rbuf, fin, ret, acc,
    w_sem, kv_local, kv_send, kv_recv, q_send, q_recv, g_sem, x_send, xs_send, f_send, x_recv,
    a_send, a_recv, r_send, r_recv, y_send, y_recv,
):
    z = lax.axis_index("seq")
    c = lax.axis_index("tp")
    sib = 1 - c
    has_left = z > 0
    has_right = z < n - 1
    end = (z == 0) | (z == n - 1)
    inner = (z > 0) & (z < n - 1)
    hosts = (z == 1) | (z == n - 2)
    guest = jnp.where(z == 1, 0, n - 1)
    host = jnp.where(z == 0, 1, n - 2)
    go_left = z > 1
    go_right = z < n - 2
    left, right, other = {"seq": z - 1}, {"seq": z + 1}, {"tp": sib}
    tokens = qbuf.shape[1]
    piece = kv_hbm.shape[2]
    groups = HEADS // KV_HEADS
    span = groups * HEAD_DIM
    width = att.shape[2]
    two = 2
    lag = KV_LAG * (n - 3) + SIB_LAG

    barrier = pltpu.get_barrier_semaphore()

    @pl.when(has_left)
    def _():
        for e in range(two):
            pl.semaphore_signal(barrier, inc=1, device_id={"seq": z - 1, "tp": e}, device_id_type=MESH)

    @pl.when(has_right)
    def _():
        for e in range(two):
            pl.semaphore_signal(barrier, inc=1, device_id={"seq": z + 1, "tp": e}, device_id_type=MESH)

    pl.semaphore_signal(barrier, inc=1, device_id=other, device_id_type=MESH)

    loads = [
        pltpu.make_async_copy(q_hbm, qbuf.at[0], w_sem.at[0]),
        pltpu.make_async_copy(wg_hbm, wg, w_sem.at[1]),
        pltpu.make_async_copy(wu_hbm, wu, w_sem.at[2]),
        pltpu.make_async_copy(wd_hbm, wd, w_sem.at[3]),
    ]
    own_kv = [
        pltpu.make_async_copy(kv_hbm.at[h], kvbuf.at[h, :, z, c], kv_local.at[h])
        for h in range(KV_HEADS)
    ]
    small = [
        pltpu.make_async_copy(routes_hbm, routes_ref, w_sem.at[4]),
        pltpu.make_async_copy(gates_hbm, gates_ref, w_sem.at[5]),
        pltpu.make_async_copy(gain_hbm, gain_ref, w_sem.at[6]),
    ]
    for copy in own_kv + small:
        copy.start()
    loads[0].start()

    for copy in own_kv + small:
        copy.wait()
    loads[0].wait()

    tri = (
        lax.broadcasted_iota(jnp.int32, (tokens, tokens), 0)
        <= lax.broadcasted_iota(jnp.int32, (tokens, tokens), 1)
    ).astype(F32)
    slots = lax.broadcasted_iota(jnp.int32, (CAP, tokens), 0).astype(F32)

    def picks(routes):
        chosen = []
        for e in range(two):
            hit = jnp.max((routes == e).astype(F32), axis=0, keepdims=True)
            rank = jnp.dot(jnp.broadcast_to(hit, (CAP, tokens)), tri, preferred_element_type=F32)
            chosen.append(jnp.where((rank - 1.0 == slots) & (hit > 0.0), 1.0, 0.0))
        return jnp.concatenate(chosen, axis=0)

    sel[0] = picks(routes_ref[...]).astype(BF16)

    pl.semaphore_wait(barrier, 1 + 2 * has_left.astype(jnp.int32) + 2 * has_right.astype(jnp.int32))

    def remote(src, dst, send, recv, device):
        return pltpu.make_async_remote_copy(
            src_ref=src, dst_ref=dst, send_sem=send, recv_sem=recv,
            device_id=device, device_id_type=MESH,
        )

    def kv_copy(h, oz, oc, way, device):
        slot = kvbuf.at[h, :, oz, oc]
        return remote(slot, slot, kv_send.at[h, oz, way], kv_recv.at[h, oz, oc], device)

    def pass_kv(h, oz, way):
        if way != 1:
            @pl.when(go_left)
            def _():
                kv_copy(h, oz, c, 0, left).start()

        if way != 0:
            @pl.when(go_right)
            def _():
                kv_copy(h, oz, c, 1, right).start()

        @pl.when(inner)
        def _():
            kv_copy(h, oz, c, 2, other).start()

    def query_copy(h):
        cols = pl.ds(pl.multiple_of(h * span, span), span)
        return remote(
            qbuf.at[0, :, cols], qbuf.at[1, :, cols], q_send.at[h], q_recv.at[h], {"seq": host}
        )

    def route_copy():
        return remote(routes_ref, groutes, g_sem.at[0], g_sem.at[1], {"seq": host})

    @pl.when(end)
    def _():
        route_copy().start()

    @pl.when(inner)
    def _():
        for h in range(LEAD):
            pass_kv(h, z, 2)

    @pl.when(end)
    def _():
        for h in range(END_LEAD):
            pass_kv(h, z, 2)
        for h in range(KV_HEADS):
            query_copy(h).start()
            if h + END_LEAD < KV_HEADS:
                pass_kv(h + END_LEAD, z, 2)

    for load in loads[1:]:
        load.start()

    @pl.when(hosts)
    def _():
        route_copy().wait_recv()
        sel[1] = picks(groutes[...]).astype(BF16)

    plen = plen_ref[0]
    keys = n * two * piece
    position = lax.broadcasted_iota(jnp.int32, (1, keys), 1)
    allowed = (position >= PROMPT) | (position < plen)

    def attend(h, s):
        base = pl.multiple_of(h * span, span)
        query = jnp.concatenate(
            [qbuf[s, :, pl.ds(base + g * HEAD_DIM, HEAD_DIM)] for g in range(groups)], axis=0
        )
        key_rows = kvbuf[h, 0].reshape(keys, HEAD_DIM)
        value_rows = kvbuf[h, 1].reshape(keys, HEAD_DIM)
        scores = lax.dot_general(
            query, key_rows, (((1,), (1,)), ((), ())), preferred_element_type=F32
        ) * (1.0 / math.sqrt(HEAD_DIM))
        scores = jnp.where(allowed, scores, masked_score)
        weights = jnp.exp(scores - jnp.max(scores, axis=1, keepdims=True))
        total = jnp.sum(weights, axis=1, keepdims=True)
        summed = jnp.dot(weights.astype(BF16), value_rows, preferred_element_type=F32)
        result = (summed / total).astype(BF16)
        for g in range(groups):
            att[s, :, pl.ds(base + g * HEAD_DIM, HEAD_DIM)] = result[g * tokens:(g + 1) * tokens]

    cut = width // ROW_CHUNKS
    per_cut = KV_HEADS // ROW_CHUNKS

    def columns(k):
        return pl.ds(pl.multiple_of(k * cut, cut), cut)

    def origin_of(s):
        return jnp.where(s == 0, z, guest)

    def row_copy(s, e, k, way):
        return remote(
            xsel.at[s, e, :, columns(k)], xbuf.at[origin_of(s), c, :, columns(k)],
            x_send.at[s, e, k, way], x_recv.at[origin_of(s), c, k],
            {"seq": z - 1 if way == 0 else z + 1, "tp": e},
        )

    def near_copy(s, k):
        return remote(
            xsel.at[s, sib, :, columns(k)], xbuf.at[origin_of(s), c, :, columns(k)],
            xs_send.at[s, k], x_recv.at[origin_of(s), c, k], other,
        )

    def far_copy(oz, oc, k, way):
        slot = xbuf.at[oz, oc, :, columns(k)]
        return remote(
            slot, slot, f_send.at[oz, oc, k], x_recv.at[oz, oc, k], left if way == 0 else right
        )

    def att_copy(k):
        return remote(
            att.at[1, :, columns(k)], att.at[0, :, columns(k)], a_send.at[k], a_recv.at[k],
            {"seq": guest},
        )

    def whole_rows(s, k):
        return k * per_cut + per_cut - 1 + lag + s * GUEST_LAG

    def start_rows(s, k, late):
        for way, edge in ((0, z == 1), (1, z == n - 2)):
            @pl.when(~edge if late else edge)
            def _():
                for e in range(two):
                    row_copy(s, e, k, way).start()

    def send_rows(r, s, k):
        picked = jnp.dot(sel[s], att[s, :, columns(k)], preferred_element_type=F32).astype(BF16)
        for e in range(two):
            xsel[s, e, :, columns(k)] = picked[e * CAP:(e + 1) * CAP]
        @pl.when((s == 1) & (r >= HOLD))
        def _():
            start_rows(s, k, True)

        @pl.when((s == 0) & inner)
        def _():
            start_rows(0, k, False)

        @pl.when((s == 1) & (k < ATT_EARLY))
        def _():
            att_copy(k).start()

        near_copy(s, k).start()
        xbuf[origin_of(s), c, :, columns(k)] = xsel[s, c, :, columns(k)]

    def relay(oz, k, ok, way):
        @pl.when(ok)
        def _():
            for oc in range(two):
                far_copy(oz, oc, k, way).wait_recv()
                far_copy(oz, oc, k, way).start()

    def relay_round(r):
        def one(k, inner_carry):
            for d in range(1, n - 2):
                due = r == jnp.maximum(whole_rows(1, k), HOLD) + ROW_LAG * d
                relay(0, k, due & (z - d == 1), 1)
                relay(n - 1, k, due & (z + d == n - 2), 0)
            return inner_carry

        lax.fori_loop(0, ROW_CHUNKS, one, 0)

    def kv_round(r, carry):
        @pl.when(r + LEAD < KV_HEADS)
        def _():
            pass_kv(r + LEAD, z, 2)

        for d in range(1, n - 1):
            h = r - KV_LAG * (d - 1)
            live = (h >= 0) & (h < KV_HEADS)

            @pl.when(live & (z - d >= 0))
            def _():
                kv_copy(h, z - d, c, 2, other).wait_recv()
                pass_kv(h, z - d, 1)

            @pl.when(live & (z + d < n))
            def _():
                kv_copy(h, z + d, c, 2, other).wait_recv()
                pass_kv(h, z + d, 0)

        @pl.when(r == HOLD)
        def _():
            for k in range(ROW_CHUNKS):
                if whole_rows(1, k) < HOLD:
                    @pl.when(hosts)
                    def _():
                        start_rows(1, k, True)

        def one(s, inner_carry):
            h = r - lag - s * GUEST_LAG

            @pl.when((h >= 0) & (h < KV_HEADS) & ((s == 0) | hosts))
            def _():
                @pl.when(s == 0)
                def _():
                    for oz in range(n):
                        kv_copy(h, oz, sib, 2, other).wait_recv()

                @pl.when(s == 1)
                def _():
                    query_copy(h).wait_recv()

                attend(h, s)

                @pl.when(h % per_cut == per_cut - 1)
                def _():
                    send_rows(r, s, h // per_cut)

            return inner_carry

        lax.fori_loop(0, two, one, 0)
        relay_round(r)
        return carry

    attend_rounds = max(KV_HEADS + lag + GUEST_LAG, HOLD + 1)
    relay_rounds = attend_rounds + ROW_LAG * (n - 3)

    @pl.when(inner)
    def _():
        lax.fori_loop(0, attend_rounds, kv_round, 0)

        def own_rows(k, carry):
            start_rows(0, k, True)
            return carry

        lax.fori_loop(0, ROW_CHUNKS, own_rows, 0)

    for load in loads[1:]:
        load.wait()

    rows_here = two * CAP
    strip = width // SUM_CHUNKS
    pairs = n // two

    def expert(first, count):
        rows = xbuf[pl.ds(first, count)].reshape(count * rows_here, width).astype(F32)
        mean_square = jnp.mean(rows * rows, axis=1, keepdims=True)
        normed = (rows * lax.rsqrt(mean_square + epsilon) * gain_ref[...]).astype(BF16)
        gate_part = jnp.dot(normed, wg[...], preferred_element_type=F32)
        up_part = jnp.dot(normed, wu[...], preferred_element_type=F32)
        hidden = (gate_part / (1.0 + jnp.exp(-gate_part)) * up_part).astype(BF16)
        for k in range(SUM_CHUNKS):
            done = jnp.dot(
                hidden, wd[:, k * strip:(k + 1) * strip], preferred_element_type=F32
            ).astype(BF16)
            for i in range(count):
                part[first + i, k] = done[i * rows_here:(i + 1) * rows_here]

    def sum_copy(way, dest, k, device):
        return remote(
            part.at[dest, k], rbuf.at[way, dest, k], r_send.at[way, dest, k], r_recv.at[way, dest, k],
            device,
        )

    def gather_rows(oz):
        here = (oz == z) | (hosts & (oz == guest))

        @pl.when(end & ~here)
        def _():
            for oc in range(two):
                for k in range(ROW_CHUNKS):
                    far_copy(oz, oc, k, 0).wait_recv()

        @pl.when(here)
        def _():
            for k in range(ROW_CHUNKS):
                far_copy(oz, sib, k, 0).wait_recv()

    def send_sums(dest, start, stop):
        @pl.when(z == 0)
        def _():
            for k in range(start, stop):
                sum_copy(0, dest, k, right).start()

        @pl.when(z == n - 1)
        def _():
            for k in range(start, stop):
                sum_copy(1, dest, k, left).start()

    near = z // two

    @pl.when(hosts)
    def _():
        for i in range(two):
            gather_rows(near * two + i)
        expert(near * two, two)

    @pl.when(inner)
    def _():
        def later(r, carry):
            relay_round(r)
            return carry

        lax.fori_loop(attend_rounds, relay_rounds, later, 0)
        for d in range(1, n - 2):
            def own_relay(k, carry):
                relay(z - d, k, z - d >= 1, 1)
                relay(z + d, k, z + d <= n - 2, 0)
                return carry

            lax.fori_loop(0, ROW_CHUNKS, own_relay, 0)

    @pl.when(hosts)
    def _():
        for k in range(ATT_EARLY, ROW_CHUNKS):
            att_copy(k).start()

    def far_step(j, carry):
        p = lax.rem(near + j // two, pairs)
        i = j % two
        oz = p * two + jnp.where(p == pairs - 1, 1 - i, i)
        closing = end & (j == n)
        oz = jnp.where(closing, z, jnp.where(end & (j == 0), host, oz))

        @pl.when(closing)
        def _():
            send_sums(host, SPLIT, SUM_CHUNKS)
            for k in range(ROW_CHUNKS):
                att_copy(k).wait_recv()
            for k in range(ROW_CHUNKS):
                send_rows(0, 0, k)

        @pl.when(closing | ((j < n) & jnp.where(hosts, j >= two, jnp.where(end, j != 1, True))))
        def _():
            gather_rows(oz)
            expert(oz, 1)

            @pl.when(j == 0)
            def _():
                send_sums(oz, 0, SPLIT)

            @pl.when((j > 0) & (j < n))
            def _():
                send_sums(oz, 0, SUM_CHUNKS)

        return carry

    lax.fori_loop(0, n + 1, far_step, 0)

    def pass_sum(way, dest, k, joins, device):
        @pl.when(joins)
        def _():
            sum_copy(way, dest, k, device).wait_recv()
            part[dest, k] = (part[dest, k].astype(F32) + rbuf[way, dest, k].astype(F32)).astype(BF16)

        sum_copy(way, dest, k, device).start()

    def sum_round(t, carry):
        i = t - SUM_LAG * z
        dest = n - 1 - i // SUM_CHUNKS

        @pl.when(inner & (i >= 0) & (dest > z))
        def _():
            pass_sum(0, dest, i % SUM_CHUNKS, has_left, right)

        i_back = t - SUM_LAG * (n - 1 - z)
        home = i_back // SUM_CHUNKS

        @pl.when(inner & (i_back >= 0) & (home < z))
        def _():
            pass_sum(1, home, i_back % SUM_CHUNKS, has_right, left)

        return carry

    lax.fori_loop(0, (SUM_CHUNKS + SUM_LAG) * (n - 1), sum_round, 0)

    def result_copy(oc, k):
        cols = pl.ds(k * strip, strip)
        return remote(fin.at[sib, :, cols], ret.at[oc, :, cols], y_send.at[k], y_recv.at[k], other)

    for k in range(SUM_CHUNKS):
        cols = slice(k * strip, (k + 1) * strip)
        acc[...] = part[z, k].astype(F32)

        @pl.when(has_left)
        def _():
            sum_copy(0, z, k, right).wait_recv()
            acc[...] += rbuf[0, z, k].astype(F32)

        @pl.when(has_right)
        def _():
            sum_copy(1, z, k, left).wait_recv()
            acc[...] += rbuf[1, z, k].astype(F32)

        fin[:, :, cols] = acc[...].astype(BF16).reshape(two, CAP, strip)
        result_copy(c, k).start()
        ret[c, :, cols] = fin[c, :, cols]

    routes = routes_ref[...]
    gates = gates_ref[...]
    select = picks(routes)
    combine = []
    for e in range(two):
        gate = jnp.sum(jnp.where(routes == e, gates, 0.0), axis=0, keepdims=True)
        combine.append(select[e * CAP:(e + 1) * CAP] * gate)
    cw = jnp.transpose(jnp.concatenate(combine, axis=0))
    first = cw.astype(BF16)
    rest = cw - first.astype(F32)
    second = rest.astype(BF16)
    third = (rest - second.astype(F32)).astype(BF16)
    for k in range(SUM_CHUNKS):
        cols = slice(k * strip, (k + 1) * strip)
        result_copy(sib, k).wait_recv()
        returned = ret[:, :, cols].reshape(rows_here, strip)
        total = (
            jnp.dot(first, returned, preferred_element_type=F32)
            + jnp.dot(second, returned, preferred_element_type=F32)
            + jnp.dot(third, returned, preferred_element_type=F32)
        )
        out_ref[:, cols] = (att[0, :, cols].astype(F32) + total).astype(BF16)

    for k in range(SUM_CHUNKS):
        result_copy(c, k).wait_send()

    def drain_kv(h, carry):
        for oz in range(n):
            @pl.when(go_left & (oz >= z))
            def _():
                kv_copy(h, oz, c, 0, left).wait_send()

            @pl.when(go_right & (oz <= z))
            def _():
                kv_copy(h, oz, c, 1, right).wait_send()

            @pl.when(inner)
            def _():
                kv_copy(h, oz, c, 2, other).wait_send()

        @pl.when(end)
        def _():
            query_copy(h).wait_send()

        return carry

    lax.fori_loop(0, KV_HEADS, drain_kv, 0)

    @pl.when(end)
    def _():
        route_copy().wait_send()

    @pl.when(hosts)
    def _():
        for k in range(ROW_CHUNKS):
            att_copy(k).wait_send()

    def drain_rows(k, carry):
        for s in range(two):
            for way, edge in ((0, z == 1), (1, z == n - 2)):
                @pl.when(inner if s == 0 else hosts & ~edge)
                def _():
                    for e in range(two):
                        row_copy(s, e, k, way).wait_send()

            @pl.when((s == 0) | hosts)
            def _():
                near_copy(s, k).wait_send()

        for oz in range(n):
            from_left = (oz < z) & ~((oz == 0) & (z == 1))
            from_right = (oz > z) & ~((oz == n - 1) & (z == n - 2))

            @pl.when(inner & (from_left | from_right))
            def _():
                for oc in range(two):
                    far_copy(oz, oc, k, 0).wait_send()

        return carry

    lax.fori_loop(0, ROW_CHUNKS, drain_rows, 0)

    for oz in range(n):
        for k in range(SUM_CHUNKS):
            @pl.when(oz > z)
            def _():
                sum_copy(0, oz, k, right).wait_send()

            @pl.when(oz < z)
            def _():
                sum_copy(1, oz, k, left).wait_send()


def body(
    queries, keys_values, prompt_lengths, routes, gate_weights, norm_gain, w_gate, w_up, w_down
):
    n = lax.axis_size("seq")
    tokens, width = queries.shape[1:]
    piece = keys_values.shape[1]
    ff = w_gate.shape[2]
    kv = keys_values[0].reshape(piece, 2, KV_HEADS, HEAD_DIM).transpose(2, 1, 0, 3)
    top = routes.shape[2]
    strip = width // SUM_CHUNKS
    vmem = pl.BlockSpec(memory_space=pltpu.VMEM)
    hbm = pl.BlockSpec(memory_space=pltpu.HBM)
    dma = pltpu.SemaphoreType.DMA
    mixed = pl.pallas_call(
        functools.partial(kernel, n),
        out_shape=jax.ShapeDtypeStruct((tokens, width), BF16),
        in_specs=[pl.BlockSpec(memory_space=pltpu.SMEM)] + [hbm] * 8,
        out_specs=vmem,
        scratch_shapes=[
            pltpu.VMEM((top, tokens), jnp.int32),
            pltpu.VMEM((top, tokens), F32),
            pltpu.VMEM((1, width), F32),
            pltpu.VMEM((2, tokens, width), BF16),
            pltpu.VMEM((width, ff), BF16),
            pltpu.VMEM((width, ff), BF16),
            pltpu.VMEM((ff, width), BF16),
            pltpu.VMEM((KV_HEADS, 2, n, 2, piece, HEAD_DIM), BF16),
            pltpu.VMEM((2, tokens, width), BF16),
            pltpu.VMEM((top, tokens), jnp.int32),
            pltpu.VMEM((2, 2 * CAP, tokens), BF16),
            pltpu.VMEM((2, 2, CAP, width), BF16),
            pltpu.VMEM((n, 2, CAP, width), BF16),
            pltpu.VMEM((n, SUM_CHUNKS, 2 * CAP, strip), BF16),
            pltpu.VMEM((2, n, SUM_CHUNKS, 2 * CAP, strip), BF16),
            pltpu.VMEM((2, CAP, width), BF16),
            pltpu.VMEM((2, CAP, width), BF16),
            pltpu.VMEM((2 * CAP, strip), F32),
            dma((7,)),
            dma((KV_HEADS,)),
            dma((KV_HEADS, n, 3)),
            dma((KV_HEADS, n, 2)),
            dma((KV_HEADS,)),
            dma((KV_HEADS,)),
            dma((2,)),
            dma((2, 2, ROW_CHUNKS, 2)),
            dma((2, ROW_CHUNKS)),
            dma((n, 2, ROW_CHUNKS)),
            dma((n, 2, ROW_CHUNKS)),
            dma((ROW_CHUNKS,)),
            dma((ROW_CHUNKS,)),
            dma((2, n, SUM_CHUNKS)),
            dma((2, n, SUM_CHUNKS)),
            dma((SUM_CHUNKS,)),
            dma((SUM_CHUNKS,)),
        ],
        compiler_params=pltpu.CompilerParams(
            collective_id=0, has_side_effects=True, vmem_limit_bytes=60 * 1024 * 1024
        ),
    )(
        prompt_lengths, kv, routes[0].T, gate_weights[0].T, norm_gain[None], queries[0],
        w_gate[0], w_up[0], w_down[0],
    )
    return mixed[None]


def solution(mesh):
    return jax.shard_map(
        body,
        mesh=mesh,
        in_specs=(
            P(("group", "exp"), ("seq", "tp"), None),
            P(("group", "exp"), ("seq", "tp"), None, None),
            P(("group", "exp")),
            P(("group", "exp"), ("seq", "tp"), None),
            P(("group", "exp"), ("seq", "tp"), None),
            P(),
            P("tp", None, "seq"),
            P("tp", None, "seq"),
            P("tp", "seq", None),
        ),
        out_specs=P(("group", "exp"), ("seq", "tp"), None),
        check_vma=False,
    )
```

```python
import functools
import math

import jax
import jax.numpy as jnp
from jax import lax
from jax.experimental import pallas as pl
from jax.experimental.pallas import tpu as pltpu
from jax.sharding import PartitionSpec as P

HEADS = 32
KV_HEADS = 8
HEAD_DIM = 128
PROMPT = 256
CAP = 16
LEAD = 2
SUM_CHUNKS = 4
ROW_CHUNKS = 4
ROW_LAG = 2
GUEST_LAG = 1
HOLD = 7
ATT_EARLY = 3
SPLIT = 2
FIRST_RELAYS = 1
END_CHUNKS = 2
KV_LAG = 2
SIB_LAG = 1
END_LEAD = 6
SUM_LAG = 3

epsilon = 1e-06
masked_score = -1e30
MESH = pl.DeviceIdType.MESH
F32 = jnp.float32
BF16 = jnp.bfloat16


def kernel(
    n, plen_ref, kv_hbm, routes_hbm, gates_hbm, gain_hbm, q_hbm, wg_hbm, wu_hbm, wd_hbm,
    out_ref,
    routes_ref, gates_ref, gain_ref, kv_raw, qbuf, wg, wu, wd, kvbuf, att, groutes, sel, xsel, xbuf, part, rbuf, fin, ret, acc,
    w_sem, kv_local, kv_send, kv_recv, q_send, q_recv, g_sem, x_send, xs_send, f_send, x_recv,
    a_send, a_recv, r_send, r_recv, y_send, y_recv,
):
    z = lax.axis_index("seq")
    c = lax.axis_index("tp")
    sib = 1 - c
    has_left = z > 0
    has_right = z < n - 1
    end = (z == 0) | (z == n - 1)
    inner = (z > 0) & (z < n - 1)
    hosts = (z == 1) | (z == n - 2)
    guest = jnp.where(z == 1, 0, n - 1)
    host = jnp.where(z == 0, 1, n - 2)
    end_heads = END_CHUNKS * KV_HEADS // ROW_CHUNKS

    def go_left(h):
        return (z > 1) | ((z == 1) & (h < end_heads))

    def go_right(h):
        return (z < n - 2) | ((z == n - 2) & (h < end_heads))

    left, right, other = {"seq": z - 1}, {"seq": z + 1}, {"tp": sib}
    tokens = qbuf.shape[1]
    piece = kv_hbm.shape[0]
    groups = HEADS // KV_HEADS
    span = groups * HEAD_DIM
    width = att.shape[2]
    two = 2
    lag = KV_LAG * (n - 3) + SIB_LAG

    barrier = pltpu.get_barrier_semaphore()

    @pl.when(has_left)
    def _():
        for e in range(two):
            pl.semaphore_signal(barrier, inc=1, device_id={"seq": z - 1, "tp": e}, device_id_type=MESH)

    @pl.when(has_right)
    def _():
        for e in range(two):
            pl.semaphore_signal(barrier, inc=1, device_id={"seq": z + 1, "tp": e}, device_id_type=MESH)

    pl.semaphore_signal(barrier, inc=1, device_id=other, device_id_type=MESH)

    loads = [
        pltpu.make_async_copy(q_hbm, qbuf.at[0], w_sem.at[0]),
        pltpu.make_async_copy(wg_hbm, wg, w_sem.at[1]),
        pltpu.make_async_copy(wu_hbm, wu, w_sem.at[2]),
        pltpu.make_async_copy(wd_hbm, wd, w_sem.at[3]),
    ]
    own_kv = pltpu.make_async_copy(kv_hbm, kv_raw, kv_local.at[0])
    small = [
        pltpu.make_async_copy(routes_hbm, routes_ref, w_sem.at[4]),
        pltpu.make_async_copy(gates_hbm, gates_ref, w_sem.at[5]),
        pltpu.make_async_copy(gain_hbm, gain_ref, w_sem.at[6]),
    ]
    own_kv.start()
    for copy in small:
        copy.start()
    loads[0].start()

    own_kv.wait()
    block = 16 if piece % 16 == 0 else 8
    lines = 2 * KV_HEADS
    row = lax.broadcasted_iota(jnp.int32, (block * lines, block * lines), 0)
    column = lax.broadcasted_iota(jnp.int32, (block * lines, block * lines), 1)
    turn = (column == (row % block) * lines + row // block).astype(BF16)
    for b in range(piece // block):
        rows = kv_raw[b * block:(b + 1) * block].reshape(block * lines, HEAD_DIM)
        turned = jnp.dot(turn, rows, preferred_element_type=F32).astype(BF16)
        for i in range(lines):
            kvbuf[i // 2, i % 2, z, c, b * block:(b + 1) * block] = turned[i * block:(i + 1) * block]
    for copy in small:
        copy.wait()
    loads[0].wait()

    tri = (
        lax.broadcasted_iota(jnp.int32, (tokens, tokens), 0)
        <= lax.broadcasted_iota(jnp.int32, (tokens, tokens), 1)
    ).astype(F32)
    slots = lax.broadcasted_iota(jnp.int32, (CAP, tokens), 0).astype(F32)

    def picks(routes):
        chosen = []
        for e in range(two):
            hit = jnp.max((routes == e).astype(F32), axis=0, keepdims=True)
            rank = jnp.dot(jnp.broadcast_to(hit, (CAP, tokens)), tri, preferred_element_type=F32)
            chosen.append(jnp.where((rank - 1.0 == slots) & (hit > 0.0), 1.0, 0.0))
        return jnp.concatenate(chosen, axis=0)

    sel[0] = picks(routes_ref[...]).astype(BF16)

    pl.semaphore_wait(barrier, 1 + 2 * has_left.astype(jnp.int32) + 2 * has_right.astype(jnp.int32))

    def remote(src, dst, send, recv, device):
        return pltpu.make_async_remote_copy(
            src_ref=src, dst_ref=dst, send_sem=send, recv_sem=recv,
            device_id=device, device_id_type=MESH,
        )

    def kv_copy(h, oz, oc, way, device):
        slot = kvbuf.at[h, :, oz, oc]
        return remote(slot, slot, kv_send.at[h, oz, way], kv_recv.at[h, oz, oc], device)

    def pass_kv(h, oz, way):
        if way != 1:
            @pl.when(go_left(h))
            def _():
                kv_copy(h, oz, c, 0, left).start()

        if way != 0:
            @pl.when(go_right(h))
            def _():
                kv_copy(h, oz, c, 1, right).start()

        @pl.when(inner | (h < end_heads))
        def _():
            kv_copy(h, oz, c, 2, other).start()

    def query_copy(h):
        cols = pl.ds(pl.multiple_of(h * span, span), span)
        return remote(
            qbuf.at[0, :, cols], qbuf.at[1, :, cols], q_send.at[h], q_recv.at[h], {"seq": host}
        )

    def route_copy():
        return remote(routes_ref, groutes, g_sem.at[0], g_sem.at[1], {"seq": host})

    @pl.when(end)
    def _():
        route_copy().start()

    @pl.when(inner)
    def _():
        for h in range(LEAD):
            pass_kv(h, z, 2)

    @pl.when(end)
    def _():
        for h in range(END_LEAD):
            pass_kv(h, z, 2)
        for h in range(min(END_LEAD, end_heads), KV_HEADS):
            if h >= end_heads:
                query_copy(h).start()
            if h + END_LEAD - end_heads in range(END_LEAD, KV_HEADS):
                pass_kv(h + END_LEAD - end_heads, z, 2)

    for load in loads[1:]:
        load.start()

    @pl.when(hosts)
    def _():
        route_copy().wait_recv()
        sel[1] = picks(groutes[...]).astype(BF16)

    plen = plen_ref[0]
    keys = n * two * piece
    position = lax.broadcasted_iota(jnp.int32, (1, keys), 1)
    allowed = (position >= PROMPT) | (position < plen)

    def attend(h, s):
        base = pl.multiple_of(h * span, span)
        query = jnp.concatenate(
            [qbuf[s, :, pl.ds(base + g * HEAD_DIM, HEAD_DIM)] for g in range(groups)], axis=0
        )
        key_rows = kvbuf[h, 0].reshape(keys, HEAD_DIM)
        value_rows = kvbuf[h, 1].reshape(keys, HEAD_DIM)
        scores = lax.dot_general(
            query, key_rows, (((1,), (1,)), ((), ())), preferred_element_type=F32
        ) * (1.0 / math.sqrt(HEAD_DIM))
        scores = jnp.where(allowed, scores, masked_score)
        weights = jnp.exp(scores - jnp.max(scores, axis=1, keepdims=True))
        total = jnp.sum(weights, axis=1, keepdims=True)
        summed = jnp.dot(weights.astype(BF16), value_rows, preferred_element_type=F32)
        result = (summed / total).astype(BF16)
        for g in range(groups):
            att[s, :, pl.ds(base + g * HEAD_DIM, HEAD_DIM)] = result[g * tokens:(g + 1) * tokens]

    cut = width // ROW_CHUNKS
    per_cut = KV_HEADS // ROW_CHUNKS

    def columns(k):
        return pl.ds(pl.multiple_of(k * cut, cut), cut)

    def origin_of(s):
        return jnp.where(s == 0, z, guest)

    def row_copy(s, e, k, way):
        return remote(
            xsel.at[s, e, :, columns(k)], xbuf.at[origin_of(s), c, :, columns(k)],
            x_send.at[s, e, k, way], x_recv.at[origin_of(s), c, k],
            {"seq": z - 1 if way == 0 else z + 1, "tp": e},
        )

    def near_copy(s, k):
        return remote(
            xsel.at[s, sib, :, columns(k)], xbuf.at[origin_of(s), c, :, columns(k)],
            xs_send.at[s, k], x_recv.at[origin_of(s), c, k], other,
        )

    def far_copy(oz, oc, k, way):
        slot = xbuf.at[oz, oc, :, columns(k)]
        return remote(
            slot, slot, f_send.at[oz, oc, k], x_recv.at[oz, oc, k], left if way == 0 else right
        )

    def att_copy(k):
        return remote(
            att.at[1, :, columns(k)], att.at[0, :, columns(k)], a_send.at[k], a_recv.at[k],
            {"seq": guest},
        )

    def whole_rows(s, k):
        return k * per_cut + per_cut - 1 + lag + s * GUEST_LAG

    def start_rows(s, k, late):
        for way, edge in ((0, z == 1), (1, z == n - 2)):
            @pl.when(~edge if late else edge)
            def _():
                for e in range(two):
                    row_copy(s, e, k, way).start()

    def send_rows(r, s, k):
        picked = jnp.dot(sel[s], att[s, :, columns(k)], preferred_element_type=F32).astype(BF16)
        for e in range(two):
            xsel[s, e, :, columns(k)] = picked[e * CAP:(e + 1) * CAP]
        @pl.when((s == 1) & (r >= HOLD))
        def _():
            start_rows(s, k, True)

        @pl.when((s == 0) & inner)
        def _():
            start_rows(0, k, False)

        for way, far_end in ((0, z == n - 1), (1, z == 0)):
            @pl.when(far_end & (k < END_CHUNKS))
            def _():
                for e in range(two):
                    row_copy(0, e, k, way).start()

        @pl.when((s == 1) & (k < ATT_EARLY))
        def _():
            att_copy(k).start()

        near_copy(s, k).start()
        xbuf[origin_of(s), c, :, columns(k)] = xsel[s, c, :, columns(k)]

    def relay(oz, k, ok, way):
        @pl.when(ok)
        def _():
            for oc in range(two):
                far_copy(oz, oc, k, way).wait_recv()
                far_copy(oz, oc, k, way).start()

    def relay_round(r):
        def one(k, inner_carry):
            from_end = whole_rows(0, k) + KV_LAG + ROW_LAG
            sent = jnp.where(k < END_CHUNKS, from_end, jnp.maximum(whole_rows(1, k), HOLD))
            handed = (k < END_CHUNKS) & (r == from_end)
            relay(0, k, handed & (z == 1), 1)
            relay(n - 1, k, handed & (z == n - 2), 0)
            for d in range(1, n - 2):
                due = r == sent + ROW_LAG * d
                relay(0, k, due & (z - d == 1), 1)
                relay(n - 1, k, due & (z + d == n - 2), 0)
            return inner_carry

        lax.fori_loop(0, ROW_CHUNKS, one, 0)

    reach = jnp.where(end, end_heads, KV_HEADS)

    def kv_round(r, carry):
        @pl.when(inner & (r + LEAD < KV_HEADS))
        def _():
            pass_kv(r + LEAD, z, 2)

        for d in range(1, n):
            h = r - KV_LAG * (d - 1)
            live = (h >= 0) & (h < reach)

            @pl.when(live & (z - d >= 0))
            def _():
                kv_copy(h, z - d, c, 2, other).wait_recv()
                pass_kv(h, z - d, 1)

            @pl.when(live & (z + d < n))
            def _():
                kv_copy(h, z + d, c, 2, other).wait_recv()
                pass_kv(h, z + d, 0)

        @pl.when(r == HOLD)
        def _():
            for k in range(END_CHUNKS, ROW_CHUNKS):
                if whole_rows(1, k) < HOLD:
                    @pl.when(hosts)
                    def _():
                        start_rows(1, k, True)

        def one(s, inner_carry):
            h = r - lag - s * GUEST_LAG - KV_LAG * end.astype(jnp.int32)

            @pl.when((h >= s * end_heads) & (h < reach) & ((s == 0) | hosts))
            def _():
                @pl.when(s == 0)
                def _():
                    for oz in range(n):
                        kv_copy(h, oz, sib, 2, other).wait_recv()

                @pl.when(s == 1)
                def _():
                    query_copy(h).wait_recv()

                attend(h, s)

                @pl.when(h % per_cut == per_cut - 1)
                def _():
                    send_rows(r, s, h // per_cut)

            return inner_carry

        lax.fori_loop(0, two, one, 0)
        relay_round(r)
        return carry

    attend_rounds = max(KV_HEADS + lag + GUEST_LAG, HOLD + 1)
    relay_rounds = attend_rounds + ROW_LAG * (n - 3)

    lax.fori_loop(0, attend_rounds, kv_round, 0)

    @pl.when(inner)
    def _():
        def own_rows(k, carry):
            start_rows(0, k, True)
            return carry

        lax.fori_loop(0, ROW_CHUNKS, own_rows, 0)

    for load in loads[1:]:
        load.wait()

    rows_here = two * CAP
    strip = width // SUM_CHUNKS
    pairs = n // two

    def sum_copy(way, dest, k, device):
        return remote(
            part.at[dest, k], rbuf.at[way, dest, k], r_send.at[way, dest, k], r_recv.at[way, dest, k],
            device,
        )

    def gather_rows(oz, k):
        here = (oz == z) | (hosts & (oz == guest))

        @pl.when(end & ~here)
        def _():
            for oc in range(two):
                far_copy(oz, oc, k, 0).wait_recv()

        @pl.when((oz == z) | (here & (k >= END_CHUNKS)))
        def _():
            far_copy(oz, sib, k, 0).wait_recv()

    def send_sum(dest, k):
        @pl.when(z == 0)
        def _():
            sum_copy(0, dest, k, right).start()

        @pl.when(z == n - 1)
        def _():
            sum_copy(1, dest, k, left).start()

    def expert(first, count, sends):
        squares, gate_part, up_part = 0.0, 0.0, 0.0
        for k in range(ROW_CHUNKS):
            for i in range(count):
                gather_rows(first + i, k)
            here = slice(k * cut, (k + 1) * cut)
            rows = xbuf[pl.ds(first, count), :, :, here].reshape(count * rows_here, cut).astype(F32)
            squares += jnp.sum(rows * rows, axis=1, keepdims=True)
            gained = (rows * gain_ref[:, here]).astype(BF16)
            gate_part += jnp.dot(gained, wg[here], preferred_element_type=F32)
            up_part += jnp.dot(gained, wu[here], preferred_element_type=F32)
        scale = lax.rsqrt(squares / width + epsilon)
        gate_part *= scale
        up_part *= scale
        hidden = (gate_part / (1.0 + jnp.exp(-gate_part)) * up_part).astype(BF16)
        for k in range(SUM_CHUNKS):
            done = jnp.dot(
                hidden, wd[:, k * strip:(k + 1) * strip], preferred_element_type=F32
            ).astype(BF16)
            for i in range(count):
                part[first + i, k] = done[i * rows_here:(i + 1) * rows_here]

            @pl.when(k < sends)
            def _():
                send_sum(first, k)

    near = z // two

    @pl.when(hosts)
    def _():
        expert(near * two, two, 0)

    def own_relays(d, start, stop):
        def one(k, carry):
            relay(z - d, k, z - d >= 1, 1)
            relay(z + d, k, z + d <= n - 2, 0)
            return carry

        lax.fori_loop(start, stop, one, 0)

    early = FIRST_RELAYS if n == 4 else ROW_CHUNKS
    begin = jnp.where(hosts, two, 0)

    def far_step(j, carry):
        p = lax.rem(near + j // two, pairs)
        i = j % two
        oz = p * two + jnp.where(p == pairs - 1, 1 - i, i)
        closing = end & (j == n)

        @pl.when(inner & (j == begin))
        def _():
            def later(r, inner_carry):
                relay_round(r)
                return inner_carry

            lax.fori_loop(attend_rounds, relay_rounds, later, 0)
            for d in range(1, n - 2):
                own_relays(d, 0, early)

        @pl.when(inner & (j == begin + 1))
        def _():
            for d in range(1, n - 2):
                own_relays(d, early, ROW_CHUNKS)

            @pl.when(hosts)
            def _():
                for k in range(max(ATT_EARLY, END_CHUNKS), ROW_CHUNKS):
                    att_copy(k).start()

        oz = jnp.where(closing, z, jnp.where(end & (j == 0), host, oz))

        @pl.when(closing)
        def _():
            for k in range(SPLIT, SUM_CHUNKS):
                send_sum(host, k)
            for k in range(END_CHUNKS, ROW_CHUNKS):
                att_copy(k).wait_recv()
                send_rows(0, 0, k)

        @pl.when(closing | ((j < n) & jnp.where(hosts, j >= two, jnp.where(end, j != 1, True))))
        def _():
            sends = jnp.where(j == 0, SPLIT, jnp.where(end & (j < n), SUM_CHUNKS, 0))
            expert(oz, 1, sends)

        return carry

    lax.fori_loop(0, n + 1, far_step, 0)

    def pass_sum(way, dest, k, joins, device):
        @pl.when(joins)
        def _():
            sum_copy(way, dest, k, device).wait_recv()
            part[dest, k] = (part[dest, k].astype(F32) + rbuf[way, dest, k].astype(F32)).astype(BF16)

        sum_copy(way, dest, k, device).start()

    def sum_round(t, carry):
        i = t - SUM_LAG * z
        dest = n - 1 - i // SUM_CHUNKS

        @pl.when(inner & (i >= 0) & (dest > z))
        def _():
            pass_sum(0, dest, i % SUM_CHUNKS, has_left, right)

        i_back = t - SUM_LAG * (n - 1 - z)
        home = i_back // SUM_CHUNKS

        @pl.when(inner & (i_back >= 0) & (home < z))
        def _():
            pass_sum(1, home, i_back % SUM_CHUNKS, has_right, left)

        return carry

    lax.fori_loop(0, (SUM_CHUNKS + SUM_LAG) * (n - 1), sum_round, 0)

    def result_copy(oc, k):
        cols = pl.ds(k * strip, strip)
        return remote(fin.at[sib, :, cols], ret.at[oc, :, cols], y_send.at[k], y_recv.at[k], other)

    for k in range(SUM_CHUNKS):
        cols = slice(k * strip, (k + 1) * strip)
        acc[...] = part[z, k].astype(F32)

        @pl.when(has_left)
        def _():
            sum_copy(0, z, k, right).wait_recv()
            acc[...] += rbuf[0, z, k].astype(F32)

        @pl.when(has_right)
        def _():
            sum_copy(1, z, k, left).wait_recv()
            acc[...] += rbuf[1, z, k].astype(F32)

        fin[:, :, cols] = acc[...].astype(BF16).reshape(two, CAP, strip)
        result_copy(c, k).start()
        ret[c, :, cols] = fin[c, :, cols]

    routes = routes_ref[...]
    gates = gates_ref[...]
    select = picks(routes)
    combine = []
    for e in range(two):
        gate = jnp.sum(jnp.where(routes == e, gates, 0.0), axis=0, keepdims=True)
        combine.append(select[e * CAP:(e + 1) * CAP] * gate)
    cw = jnp.transpose(jnp.concatenate(combine, axis=0))
    first = cw.astype(BF16)
    rest = cw - first.astype(F32)
    second = rest.astype(BF16)
    third = (rest - second.astype(F32)).astype(BF16)
    for k in range(SUM_CHUNKS):
        cols = slice(k * strip, (k + 1) * strip)
        result_copy(sib, k).wait_recv()
        returned = ret[:, :, cols].reshape(rows_here, strip)
        total = (
            jnp.dot(first, returned, preferred_element_type=F32)
            + jnp.dot(second, returned, preferred_element_type=F32)
            + jnp.dot(third, returned, preferred_element_type=F32)
        )
        out_ref[:, cols] = (att[0, :, cols].astype(F32) + total).astype(BF16)

    for k in range(SUM_CHUNKS):
        result_copy(c, k).wait_send()

    def drain_kv(h, carry):
        for oz in range(n):
            @pl.when(go_left(h) & (oz >= z))
            def _():
                kv_copy(h, oz, c, 0, left).wait_send()

            @pl.when(go_right(h) & (oz <= z))
            def _():
                kv_copy(h, oz, c, 1, right).wait_send()

            @pl.when(inner | (h < end_heads))
            def _():
                kv_copy(h, oz, c, 2, other).wait_send()

        @pl.when(end & (h >= end_heads))
        def _():
            query_copy(h).wait_send()

        return carry

    lax.fori_loop(0, KV_HEADS, drain_kv, 0)

    @pl.when(end)
    def _():
        route_copy().wait_send()

    @pl.when(hosts)
    def _():
        for k in range(END_CHUNKS, ROW_CHUNKS):
            att_copy(k).wait_send()

    def drain_rows(k, carry):
        for s in range(two):
            for way, edge, mine in ((0, z == 1, z == n - 1), (1, z == n - 2, z == 0)):
                to_host = mine & (k < END_CHUNKS)

                @pl.when(inner | to_host if s == 0 else hosts & ~edge & (k >= END_CHUNKS))
                def _():
                    for e in range(two):
                        row_copy(s, e, k, way).wait_send()

            @pl.when((s == 0) | (hosts & (k >= END_CHUNKS)))
            def _():
                near_copy(s, k).wait_send()

        for oz in range(n):
            from_left = (oz < z) & ~((oz == 0) & (z == 1))
            from_right = (oz > z) & ~((oz == n - 1) & (z == n - 2))

            handed = hosts & (oz == guest) & (k < END_CHUNKS)

            @pl.when(inner & (from_left | from_right | handed))
            def _():
                for oc in range(two):
                    far_copy(oz, oc, k, 0).wait_send()

        return carry

    lax.fori_loop(0, ROW_CHUNKS, drain_rows, 0)

    for oz in range(n):
        for k in range(SUM_CHUNKS):
            @pl.when(oz > z)
            def _():
                sum_copy(0, oz, k, right).wait_send()

            @pl.when(oz < z)
            def _():
                sum_copy(1, oz, k, left).wait_send()


def body(
    queries, keys_values, prompt_lengths, routes, gate_weights, norm_gain, w_gate, w_up, w_down
):
    n = lax.axis_size("seq")
    tokens, width = queries.shape[1:]
    piece = keys_values.shape[1]
    ff = w_gate.shape[2]
    kv = keys_values[0].reshape(piece, 2, KV_HEADS, HEAD_DIM).transpose(0, 2, 1, 3)
    kv = kv.reshape(piece, 2 * KV_HEADS, HEAD_DIM)
    top = routes.shape[2]
    strip = width // SUM_CHUNKS
    vmem = pl.BlockSpec(memory_space=pltpu.VMEM)
    hbm = pl.BlockSpec(memory_space=pltpu.HBM)
    dma = pltpu.SemaphoreType.DMA
    mixed = pl.pallas_call(
        functools.partial(kernel, n),
        out_shape=jax.ShapeDtypeStruct((tokens, width), BF16),
        in_specs=[pl.BlockSpec(memory_space=pltpu.SMEM)] + [hbm] * 8,
        out_specs=vmem,
        scratch_shapes=[
            pltpu.VMEM((top, tokens), jnp.int32),
            pltpu.VMEM((top, tokens), F32),
            pltpu.VMEM((1, width), F32),
            pltpu.VMEM((piece, 2 * KV_HEADS, HEAD_DIM), BF16),
            pltpu.VMEM((2, tokens, width), BF16),
            pltpu.VMEM((width, ff), BF16),
            pltpu.VMEM((width, ff), BF16),
            pltpu.VMEM((ff, width), BF16),
            pltpu.VMEM((KV_HEADS, 2, n, 2, piece, HEAD_DIM), BF16),
            pltpu.VMEM((2, tokens, width), BF16),
            pltpu.VMEM((top, tokens), jnp.int32),
            pltpu.VMEM((2, 2 * CAP, tokens), BF16),
            pltpu.VMEM((2, 2, CAP, width), BF16),
            pltpu.VMEM((n, 2, CAP, width), BF16),
            pltpu.VMEM((n, SUM_CHUNKS, 2 * CAP, strip), BF16),
            pltpu.VMEM((2, n, SUM_CHUNKS, 2 * CAP, strip), BF16),
            pltpu.VMEM((2, CAP, width), BF16),
            pltpu.VMEM((2, CAP, width), BF16),
            pltpu.VMEM((2 * CAP, strip), F32),
            dma((7,)),
            dma((1,)),
            dma((KV_HEADS, n, 3)),
            dma((KV_HEADS, n, 2)),
            dma((KV_HEADS,)),
            dma((KV_HEADS,)),
            dma((2,)),
            dma((2, 2, ROW_CHUNKS, 2)),
            dma((2, ROW_CHUNKS)),
            dma((n, 2, ROW_CHUNKS)),
            dma((n, 2, ROW_CHUNKS)),
            dma((ROW_CHUNKS,)),
            dma((ROW_CHUNKS,)),
            dma((2, n, SUM_CHUNKS)),
            dma((2, n, SUM_CHUNKS)),
            dma((SUM_CHUNKS,)),
            dma((SUM_CHUNKS,)),
        ],
        compiler_params=pltpu.CompilerParams(
            collective_id=0, has_side_effects=True, vmem_limit_bytes=60 * 1024 * 1024
        ),
    )(
        prompt_lengths, kv, routes[0].T, gate_weights[0].T, norm_gain[None], queries[0],
        w_gate[0], w_up[0], w_down[0],
    )
    return mixed[None]


def solution(mesh):
    return jax.shard_map(
        body,
        mesh=mesh,
        in_specs=(
            P(("group", "exp"), ("seq", "tp"), None),
            P(("group", "exp"), ("seq", "tp"), None, None),
            P(("group", "exp")),
            P(("group", "exp"), ("seq", "tp"), None),
            P(("group", "exp"), ("seq", "tp"), None),
            P(),
            P("tp", None, "seq"),
            P("tp", None, "seq"),
            P("tp", "seq", None),
        ),
        out_specs=P(("group", "exp"), ("seq", "tp"), None),
        check_vma=False,
    )
```

```python
import functools
import math

import jax
import jax.numpy as jnp
from jax import lax
from jax.experimental import pallas as pl
from jax.experimental.pallas import tpu as pltpu
from jax.sharding import PartitionSpec as P

HEADS = 32
KV_HEADS = 8
HEAD_DIM = 128
PROMPT = 256
CAP = 16
LEAD = 2
SUM_CHUNKS = 4
ROW_CHUNKS = 4
ROW_LAG = 2
GUEST_LAG = 1
HOLD = 7
ATT_EARLY = 3
SPLIT = 2
FIRST_RELAYS = 1
END_CHUNKS = 2
KV_LAG = 2
SIB_LAG = 1
END_LEAD = 6
SUM_LAG = 3

epsilon = 1e-06
masked_score = -1e30
MESH = pl.DeviceIdType.MESH
F32 = jnp.float32
BF16 = jnp.bfloat16


def kernel(
    n, plen_ref, kv_hbm, routes_hbm, gates_hbm, gain_hbm, q_hbm, wg_hbm, wu_hbm, wd_hbm,
    out_ref,
    routes_ref, gates_ref, gain_ref, kv_raw, qbuf, wg, wu, wd, kvbuf, att, groutes, sel, xsel, xbuf, part, rbuf, fin, ret, acc,
    w_sem, kv_local, kv_send, kv_recv, q_send, q_recv, g_sem, x_send, xs_send, f_send, x_recv,
    a_send, a_recv, r_send, r_recv, y_send, y_recv,
):
    z = lax.axis_index("seq")
    c = lax.axis_index("tp")
    sib = 1 - c
    has_left = z > 0
    has_right = z < n - 1
    end = (z == 0) | (z == n - 1)
    inner = (z > 0) & (z < n - 1)
    hosts = (z == 1) | (z == n - 2)
    guest = jnp.where(z == 1, 0, n - 1)
    host = jnp.where(z == 0, 1, n - 2)
    end_heads = END_CHUNKS * KV_HEADS // ROW_CHUNKS

    def go_left(h):
        return (z > 1) | ((z == 1) & (h < end_heads))

    def go_right(h):
        return (z < n - 2) | ((z == n - 2) & (h < end_heads))

    left, right, other = {"seq": z - 1}, {"seq": z + 1}, {"tp": sib}
    tokens = qbuf.shape[1]
    piece = kv_hbm.shape[0]
    groups = HEADS // KV_HEADS
    span = groups * HEAD_DIM
    width = att.shape[2]
    two = 2
    lag = KV_LAG * (n - 3) + SIB_LAG

    barrier = pltpu.get_barrier_semaphore()

    @pl.when(has_left)
    def _():
        for e in range(two):
            pl.semaphore_signal(barrier, inc=1, device_id={"seq": z - 1, "tp": e}, device_id_type=MESH)

    @pl.when(has_right)
    def _():
        for e in range(two):
            pl.semaphore_signal(barrier, inc=1, device_id={"seq": z + 1, "tp": e}, device_id_type=MESH)

    pl.semaphore_signal(barrier, inc=1, device_id=other, device_id_type=MESH)

    loads = [
        pltpu.make_async_copy(q_hbm, qbuf.at[0], w_sem.at[0]),
        pltpu.make_async_copy(wg_hbm, wg, w_sem.at[1]),
        pltpu.make_async_copy(wu_hbm, wu, w_sem.at[2]),
        pltpu.make_async_copy(wd_hbm, wd, w_sem.at[3]),
    ]
    own_kv = pltpu.make_async_copy(kv_hbm, kv_raw, kv_local.at[0])
    small = [
        pltpu.make_async_copy(routes_hbm, routes_ref, w_sem.at[4]),
        pltpu.make_async_copy(gates_hbm, gates_ref, w_sem.at[5]),
        pltpu.make_async_copy(gain_hbm, gain_ref, w_sem.at[6]),
    ]
    own_kv.start()
    for copy in small:
        copy.start()
    loads[0].start()

    own_kv.wait()
    block = 16 if piece % 16 == 0 else 8
    lines = 2 * KV_HEADS
    row = lax.broadcasted_iota(jnp.int32, (block * lines, block * lines), 0)
    column = lax.broadcasted_iota(jnp.int32, (block * lines, block * lines), 1)
    turn = (column == (row % block) * lines + row // block).astype(BF16)
    for b in range(piece // block):
        rows = kv_raw[b * block:(b + 1) * block].reshape(block * lines, HEAD_DIM)
        turned = jnp.dot(turn, rows, preferred_element_type=F32).astype(BF16)
        for i in range(lines):
            kvbuf[i // 2, i % 2, z, c, b * block:(b + 1) * block] = turned[i * block:(i + 1) * block]
    for copy in small:
        copy.wait()
    loads[0].wait()

    tri = (
        lax.broadcasted_iota(jnp.int32, (tokens, tokens), 0)
        <= lax.broadcasted_iota(jnp.int32, (tokens, tokens), 1)
    ).astype(F32)
    slots = lax.broadcasted_iota(jnp.int32, (CAP, tokens), 0).astype(F32)

    def picks(routes):
        chosen = []
        for e in range(two):
            hit = jnp.max((routes == e).astype(F32), axis=0, keepdims=True)
            rank = jnp.dot(jnp.broadcast_to(hit, (CAP, tokens)), tri, preferred_element_type=F32)
            chosen.append(jnp.where((rank - 1.0 == slots) & (hit > 0.0), 1.0, 0.0))
        return jnp.concatenate(chosen, axis=0)

    sel[0] = picks(routes_ref[...]).astype(BF16)

    pl.semaphore_wait(barrier, 1 + 2 * has_left.astype(jnp.int32) + 2 * has_right.astype(jnp.int32))

    def remote(src, dst, send, recv, device):
        return pltpu.make_async_remote_copy(
            src_ref=src, dst_ref=dst, send_sem=send, recv_sem=recv,
            device_id=device, device_id_type=MESH,
        )

    def kv_copy(h, oz, oc, way, device):
        slot = kvbuf.at[h, :, oz, oc]
        return remote(slot, slot, kv_send.at[h, oz, way], kv_recv.at[h, oz, oc], device)

    def pass_kv(h, oz, way):
        if way != 1:
            @pl.when(go_left(h))
            def _():
                kv_copy(h, oz, c, 0, left).start()

        if way != 0:
            @pl.when(go_right(h))
            def _():
                kv_copy(h, oz, c, 1, right).start()

        @pl.when(inner | (h < end_heads))
        def _():
            kv_copy(h, oz, c, 2, other).start()

    def query_copy(h):
        cols = pl.ds(pl.multiple_of(h * span, span), span)
        return remote(
            qbuf.at[0, :, cols], qbuf.at[1, :, cols], q_send.at[h], q_recv.at[h], {"seq": host}
        )

    def route_copy():
        return remote(routes_ref, groutes, g_sem.at[0], g_sem.at[1], {"seq": host})

    @pl.when(end)
    def _():
        route_copy().start()

    @pl.when(inner)
    def _():
        for h in range(LEAD):
            pass_kv(h, z, 2)

    @pl.when(end)
    def _():
        for h in range(END_LEAD):
            pass_kv(h, z, 2)
        for h in range(min(END_LEAD, end_heads), KV_HEADS):
            if h >= end_heads:
                query_copy(h).start()
            if h + END_LEAD - end_heads in range(END_LEAD, KV_HEADS):
                pass_kv(h + END_LEAD - end_heads, z, 2)

    for load in loads[1:]:
        load.start()

    @pl.when(hosts)
    def _():
        route_copy().wait_recv()
        sel[1] = picks(groutes[...]).astype(BF16)

    plen = plen_ref[0]
    keys = n * two * piece
    position = lax.broadcasted_iota(jnp.int32, (1, keys), 1)
    allowed = (position >= PROMPT) | (position < plen)

    def attend(h, s):
        base = pl.multiple_of(h * span, span)
        query = jnp.concatenate(
            [qbuf[s, :, pl.ds(base + g * HEAD_DIM, HEAD_DIM)] for g in range(groups)], axis=0
        )
        key_rows = kvbuf[h, 0].reshape(keys, HEAD_DIM)
        value_rows = kvbuf[h, 1].reshape(keys, HEAD_DIM)
        scores = lax.dot_general(
            query, key_rows, (((1,), (1,)), ((), ())), preferred_element_type=F32
        ) * (1.0 / math.sqrt(HEAD_DIM))
        scores = jnp.where(allowed, scores, masked_score)
        weights = jnp.exp(scores - jnp.max(scores, axis=1, keepdims=True))
        total = jnp.sum(weights, axis=1, keepdims=True)
        summed = jnp.dot(weights.astype(BF16), value_rows, preferred_element_type=F32)
        result = (summed / total).astype(BF16)
        for g in range(groups):
            att[s, :, pl.ds(base + g * HEAD_DIM, HEAD_DIM)] = result[g * tokens:(g + 1) * tokens]

    cut = width // ROW_CHUNKS
    per_cut = KV_HEADS // ROW_CHUNKS

    def columns(k):
        return pl.ds(pl.multiple_of(k * cut, cut), cut)

    def origin_of(s):
        return jnp.where(s == 0, z, guest)

    def row_copy(s, e, k, way):
        return remote(
            xsel.at[s, e, :, columns(k)], xbuf.at[origin_of(s), c, :, columns(k)],
            x_send.at[s, e, k, way], x_recv.at[origin_of(s), c, k],
            {"seq": z - 1 if way == 0 else z + 1, "tp": e},
        )

    def near_copy(s, k):
        return remote(
            xsel.at[s, sib, :, columns(k)], xbuf.at[origin_of(s), c, :, columns(k)],
            xs_send.at[s, k], x_recv.at[origin_of(s), c, k], other,
        )

    def far_copy(oz, oc, k, way):
        slot = xbuf.at[oz, oc, :, columns(k)]
        return remote(
            slot, slot, f_send.at[oz, oc, k], x_recv.at[oz, oc, k], left if way == 0 else right
        )

    def att_copy(k):
        return remote(
            att.at[1, :, columns(k)], att.at[0, :, columns(k)], a_send.at[k], a_recv.at[k],
            {"seq": guest},
        )

    def whole_rows(s, k):
        return k * per_cut + per_cut - 1 + lag + s * GUEST_LAG

    def start_rows(s, k, late):
        for way, edge in ((0, z == 1), (1, z == n - 2)):
            @pl.when(~edge if late else edge)
            def _():
                for e in range(two):
                    row_copy(s, e, k, way).start()

    def send_rows(r, s, k):
        picked = jnp.dot(sel[s], att[s, :, columns(k)], preferred_element_type=F32).astype(BF16)
        for e in range(two):
            xsel[s, e, :, columns(k)] = picked[e * CAP:(e + 1) * CAP]
        @pl.when((s == 1) & (r >= HOLD))
        def _():
            start_rows(s, k, True)

        @pl.when((s == 0) & inner)
        def _():
            start_rows(0, k, False)

        for way, far_end in ((0, z == n - 1), (1, z == 0)):
            @pl.when(far_end & (k < END_CHUNKS))
            def _():
                for e in range(two):
                    row_copy(0, e, k, way).start()

        @pl.when((s == 1) & (k < ATT_EARLY))
        def _():
            att_copy(k).start()

        near_copy(s, k).start()
        xbuf[origin_of(s), c, :, columns(k)] = xsel[s, c, :, columns(k)]

    def relay(oz, k, ok, way):
        @pl.when(ok)
        def _():
            for oc in range(two):
                far_copy(oz, oc, k, way).wait_recv()
                far_copy(oz, oc, k, way).start()

    def relay_round(r):
        def one(k, inner_carry):
            from_end = whole_rows(0, k) + KV_LAG + ROW_LAG
            sent = jnp.where(k < END_CHUNKS, from_end, jnp.maximum(whole_rows(1, k), HOLD))
            handed = (k < END_CHUNKS) & (r == from_end)
            relay(0, k, handed & (z == 1), 1)
            relay(n - 1, k, handed & (z == n - 2), 0)
            for d in range(1, n - 2):
                due = r == sent + ROW_LAG * d
                relay(0, k, due & (z - d == 1), 1)
                relay(n - 1, k, due & (z + d == n - 2), 0)
            return inner_carry

        lax.fori_loop(0, ROW_CHUNKS, one, 0)

    reach = jnp.where(end, end_heads, KV_HEADS)

    def kv_round(r, carry):
        @pl.when(inner & (r + LEAD < KV_HEADS))
        def _():
            pass_kv(r + LEAD, z, 2)

        for d in range(1, n):
            h = r - KV_LAG * (d - 1)
            live = (h >= 0) & (h < reach)

            @pl.when(live & (z - d >= 0))
            def _():
                kv_copy(h, z - d, c, 2, other).wait_recv()
                pass_kv(h, z - d, 1)

            @pl.when(live & (z + d < n))
            def _():
                kv_copy(h, z + d, c, 2, other).wait_recv()
                pass_kv(h, z + d, 0)

        @pl.when(r == HOLD)
        def _():
            for k in range(END_CHUNKS, ROW_CHUNKS):
                if whole_rows(1, k) < HOLD:
                    @pl.when(hosts)
                    def _():
                        start_rows(1, k, True)

        def one(s, inner_carry):
            h = r - lag - s * GUEST_LAG - KV_LAG * end.astype(jnp.int32)

            @pl.when((h >= s * end_heads) & (h < reach) & ((s == 0) | hosts))
            def _():
                @pl.when(s == 0)
                def _():
                    for oz in range(n):
                        kv_copy(h, oz, sib, 2, other).wait_recv()

                @pl.when(s == 1)
                def _():
                    query_copy(h).wait_recv()

                attend(h, s)

                @pl.when(h % per_cut == per_cut - 1)
                def _():
                    send_rows(r, s, h // per_cut)

            return inner_carry

        lax.fori_loop(0, two, one, 0)
        relay_round(r)
        return carry

    attend_rounds = max(KV_HEADS + lag + GUEST_LAG, HOLD + 1)
    relay_rounds = attend_rounds + ROW_LAG * (n - 3)

    lax.fori_loop(0, attend_rounds, kv_round, 0)

    @pl.when(inner)
    def _():
        def own_rows(k, carry):
            start_rows(0, k, True)
            return carry

        lax.fori_loop(0, ROW_CHUNKS, own_rows, 0)

    def drain_kv(h, carry):
        for oz in range(n):
            @pl.when(go_left(h) & (oz >= z))
            def _():
                kv_copy(h, oz, c, 0, left).wait_send()

            @pl.when(go_right(h) & (oz <= z))
            def _():
                kv_copy(h, oz, c, 1, right).wait_send()

            @pl.when(inner | (h < end_heads))
            def _():
                kv_copy(h, oz, c, 2, other).wait_send()

        @pl.when(end & (h >= end_heads))
        def _():
            query_copy(h).wait_send()

        return carry

    @pl.when(end)
    def _():
        lax.fori_loop(0, KV_HEADS, drain_kv, 0)
        route_copy().wait_send()

    for load in loads[1:]:
        load.wait()

    rows_here = two * CAP
    strip = width // SUM_CHUNKS
    pairs = n // two

    def sum_copy(way, dest, k, device):
        return remote(
            part.at[dest, k], rbuf.at[way, dest, k], r_send.at[way, dest, k], r_recv.at[way, dest, k],
            device,
        )

    def gather_rows(oz, k):
        here = (oz == z) | (hosts & (oz == guest))

        @pl.when(end & ~here)
        def _():
            for oc in range(two):
                far_copy(oz, oc, k, 0).wait_recv()

        @pl.when((oz == z) | (here & (k >= END_CHUNKS)))
        def _():
            far_copy(oz, sib, k, 0).wait_recv()

    def send_sum(dest, k):
        @pl.when(z == 0)
        def _():
            sum_copy(0, dest, k, right).start()

        @pl.when(z == n - 1)
        def _():
            sum_copy(1, dest, k, left).start()

    def expert(first, count, sends):
        squares, gate_part, up_part = 0.0, 0.0, 0.0
        for k in range(ROW_CHUNKS):
            for i in range(count):
                gather_rows(first + i, k)
            here = slice(k * cut, (k + 1) * cut)
            rows = xbuf[pl.ds(first, count), :, :, here].reshape(count * rows_here, cut).astype(F32)
            squares += jnp.sum(rows * rows, axis=1, keepdims=True)
            gained = (rows * gain_ref[:, here]).astype(BF16)
            gate_part += jnp.dot(gained, wg[here], preferred_element_type=F32)
            up_part += jnp.dot(gained, wu[here], preferred_element_type=F32)
        scale = lax.rsqrt(squares / width + epsilon)
        gate_part *= scale
        up_part *= scale
        hidden = (gate_part / (1.0 + jnp.exp(-gate_part)) * up_part).astype(BF16)
        for k in range(SUM_CHUNKS):
            done = jnp.dot(
                hidden, wd[:, k * strip:(k + 1) * strip], preferred_element_type=F32
            ).astype(BF16)
            for i in range(count):
                part[first + i, k] = done[i * rows_here:(i + 1) * rows_here]

            @pl.when(k < sends)
            def _():
                send_sum(first, k)

    near = z // two

    @pl.when(hosts)
    def _():
        expert(near * two, two, 0)

    def own_relays(d, start, stop):
        def one(k, carry):
            relay(z - d, k, z - d >= 1, 1)
            relay(z + d, k, z + d <= n - 2, 0)
            return carry

        lax.fori_loop(start, stop, one, 0)

    early = FIRST_RELAYS if n == 4 else ROW_CHUNKS
    begin = jnp.where(hosts, two, 0)

    def far_step(j, carry):
        p = lax.rem(near + j // two, pairs)
        i = j % two
        oz = p * two + jnp.where(p == pairs - 1, 1 - i, i)
        closing = end & (j == n)

        @pl.when(inner & (j == begin))
        def _():
            def later(r, inner_carry):
                relay_round(r)
                return inner_carry

            lax.fori_loop(attend_rounds, relay_rounds, later, 0)
            for d in range(1, n - 2):
                own_relays(d, 0, early)

        @pl.when(inner & (j == begin + 1))
        def _():
            for d in range(1, n - 2):
                own_relays(d, early, ROW_CHUNKS)

            @pl.when(hosts)
            def _():
                for k in range(max(ATT_EARLY, END_CHUNKS), ROW_CHUNKS):
                    att_copy(k).start()

        oz = jnp.where(closing, z, jnp.where(end & (j == 0), host, oz))

        @pl.when(inner & (j == begin + 1))
        def _():
            lax.fori_loop(0, KV_HEADS, drain_kv, 0)

        @pl.when(closing)
        def _():
            for k in range(SPLIT, SUM_CHUNKS):
                send_sum(host, k)
            for k in range(END_CHUNKS, ROW_CHUNKS):
                att_copy(k).wait_recv()
                send_rows(0, 0, k)

        @pl.when(closing | ((j < n) & jnp.where(hosts, j >= two, jnp.where(end, j != 1, True))))
        def _():
            sends = jnp.where(j == 0, SPLIT, jnp.where(end & (j < n), SUM_CHUNKS, 0))
            expert(oz, 1, sends)

        return carry

    lax.fori_loop(0, n + 1, far_step, 0)

    routes = routes_ref[...]
    gates = gates_ref[...]
    select = picks(routes)
    combine = []
    for e in range(two):
        gate = jnp.sum(jnp.where(routes == e, gates, 0.0), axis=0, keepdims=True)
        combine.append(select[e * CAP:(e + 1) * CAP] * gate)
    cw = jnp.transpose(jnp.concatenate(combine, axis=0))
    first = cw.astype(BF16)
    rest = cw - first.astype(F32)
    second = rest.astype(BF16)
    third = (rest - second.astype(F32)).astype(BF16)
    def pass_sum(way, dest, k, joins, device):
        @pl.when(joins)
        def _():
            sum_copy(way, dest, k, device).wait_recv()
            part[dest, k] = (part[dest, k].astype(F32) + rbuf[way, dest, k].astype(F32)).astype(BF16)

        sum_copy(way, dest, k, device).start()

    def sum_round(t, carry):
        i = t - SUM_LAG * z
        dest = n - 1 - i // SUM_CHUNKS

        @pl.when(inner & (i >= 0) & (dest > z))
        def _():
            pass_sum(0, dest, i % SUM_CHUNKS, has_left, right)

        i_back = t - SUM_LAG * (n - 1 - z)
        home = i_back // SUM_CHUNKS

        @pl.when(inner & (i_back >= 0) & (home < z))
        def _():
            pass_sum(1, home, i_back % SUM_CHUNKS, has_right, left)

        return carry

    lax.fori_loop(0, (SUM_CHUNKS + SUM_LAG) * (n - 1), sum_round, 0)

    @pl.when(hosts)
    def _():
        for k in range(END_CHUNKS, ROW_CHUNKS):
            att_copy(k).wait_send()

    def drain_rows(k, carry):
        for s in range(two):
            for way, edge, mine in ((0, z == 1, z == n - 1), (1, z == n - 2, z == 0)):
                to_host = mine & (k < END_CHUNKS)

                @pl.when(inner | to_host if s == 0 else hosts & ~edge & (k >= END_CHUNKS))
                def _():
                    for e in range(two):
                        row_copy(s, e, k, way).wait_send()

            @pl.when((s == 0) | (hosts & (k >= END_CHUNKS)))
            def _():
                near_copy(s, k).wait_send()

        for oz in range(n):
            from_left = (oz < z) & ~((oz == 0) & (z == 1))
            from_right = (oz > z) & ~((oz == n - 1) & (z == n - 2))

            handed = hosts & (oz == guest) & (k < END_CHUNKS)

            @pl.when(inner & (from_left | from_right | handed))
            def _():
                for oc in range(two):
                    far_copy(oz, oc, k, 0).wait_send()

        return carry

    lax.fori_loop(0, ROW_CHUNKS, drain_rows, 0)

    def result_copy(oc, k):
        cols = pl.ds(k * strip, strip)
        return remote(fin.at[sib, :, cols], ret.at[oc, :, cols], y_send.at[k], y_recv.at[k], other)

    for k in range(SUM_CHUNKS):
        cols = slice(k * strip, (k + 1) * strip)
        acc[...] = part[z, k].astype(F32)

        @pl.when(has_left)
        def _():
            sum_copy(0, z, k, right).wait_recv()
            acc[...] += rbuf[0, z, k].astype(F32)

        @pl.when(has_right)
        def _():
            sum_copy(1, z, k, left).wait_recv()
            acc[...] += rbuf[1, z, k].astype(F32)

        fin[:, :, cols] = acc[...].astype(BF16).reshape(two, CAP, strip)
        result_copy(c, k).start()
        ret[c, :, cols] = fin[c, :, cols]

    for k in range(SUM_CHUNKS):
        cols = slice(k * strip, (k + 1) * strip)
        result_copy(sib, k).wait_recv()
        returned = ret[:, :, cols].reshape(rows_here, strip)
        total = (
            jnp.dot(first, returned, preferred_element_type=F32)
            + jnp.dot(second, returned, preferred_element_type=F32)
            + jnp.dot(third, returned, preferred_element_type=F32)
        )
        out_ref[:, cols] = (att[0, :, cols].astype(F32) + total).astype(BF16)

    for k in range(SUM_CHUNKS):
        result_copy(c, k).wait_send()

    for oz in range(n):
        for k in range(SUM_CHUNKS):
            @pl.when(oz > z)
            def _():
                sum_copy(0, oz, k, right).wait_send()

            @pl.when(oz < z)
            def _():
                sum_copy(1, oz, k, left).wait_send()


def body(
    queries, keys_values, prompt_lengths, routes, gate_weights, norm_gain, w_gate, w_up, w_down
):
    n = lax.axis_size("seq")
    tokens, width = queries.shape[1:]
    piece = keys_values.shape[1]
    ff = w_gate.shape[2]
    kv = keys_values[0].reshape(piece, 2, KV_HEADS, HEAD_DIM).transpose(0, 2, 1, 3)
    kv = kv.reshape(piece, 2 * KV_HEADS, HEAD_DIM)
    top = routes.shape[2]
    strip = width // SUM_CHUNKS
    vmem = pl.BlockSpec(memory_space=pltpu.VMEM)
    hbm = pl.BlockSpec(memory_space=pltpu.HBM)
    dma = pltpu.SemaphoreType.DMA
    mixed = pl.pallas_call(
        functools.partial(kernel, n),
        out_shape=jax.ShapeDtypeStruct((tokens, width), BF16),
        in_specs=[pl.BlockSpec(memory_space=pltpu.SMEM)] + [hbm] * 8,
        out_specs=vmem,
        scratch_shapes=[
            pltpu.VMEM((top, tokens), jnp.int32),
            pltpu.VMEM((top, tokens), F32),
            pltpu.VMEM((1, width), F32),
            pltpu.VMEM((piece, 2 * KV_HEADS, HEAD_DIM), BF16),
            pltpu.VMEM((2, tokens, width), BF16),
            pltpu.VMEM((width, ff), BF16),
            pltpu.VMEM((width, ff), BF16),
            pltpu.VMEM((ff, width), BF16),
            pltpu.VMEM((KV_HEADS, 2, n, 2, piece, HEAD_DIM), BF16),
            pltpu.VMEM((2, tokens, width), BF16),
            pltpu.VMEM((top, tokens), jnp.int32),
            pltpu.VMEM((2, 2 * CAP, tokens), BF16),
            pltpu.VMEM((2, 2, CAP, width), BF16),
            pltpu.VMEM((n, 2, CAP, width), BF16),
            pltpu.VMEM((n, SUM_CHUNKS, 2 * CAP, strip), BF16),
            pltpu.VMEM((2, n, SUM_CHUNKS, 2 * CAP, strip), BF16),
            pltpu.VMEM((2, CAP, width), BF16),
            pltpu.VMEM((2, CAP, width), BF16),
            pltpu.VMEM((2 * CAP, strip), F32),
            dma((7,)),
            dma((1,)),
            dma((KV_HEADS, n, 3)),
            dma((KV_HEADS, n, 2)),
            dma((KV_HEADS,)),
            dma((KV_HEADS,)),
            dma((2,)),
            dma((2, 2, ROW_CHUNKS, 2)),
            dma((2, ROW_CHUNKS)),
            dma((n, 2, ROW_CHUNKS)),
            dma((n, 2, ROW_CHUNKS)),
            dma((ROW_CHUNKS,)),
            dma((ROW_CHUNKS,)),
            dma((2, n, SUM_CHUNKS)),
            dma((2, n, SUM_CHUNKS)),
            dma((SUM_CHUNKS,)),
            dma((SUM_CHUNKS,)),
        ],
        compiler_params=pltpu.CompilerParams(
            collective_id=0, has_side_effects=True, vmem_limit_bytes=60 * 1024 * 1024
        ),
    )(
        prompt_lengths, kv, routes[0].T, gate_weights[0].T, norm_gain[None], queries[0],
        w_gate[0], w_up[0], w_down[0],
    )
    return mixed[None]


def solution(mesh):
    return jax.shard_map(
        body,
        mesh=mesh,
        in_specs=(
            P(("group", "exp"), ("seq", "tp"), None),
            P(("group", "exp"), ("seq", "tp"), None, None),
            P(("group", "exp")),
            P(("group", "exp"), ("seq", "tp"), None),
            P(("group", "exp"), ("seq", "tp"), None),
            P(),
            P("tp", None, "seq"),
            P("tp", None, "seq"),
            P("tp", "seq", None),
        ),
        out_specs=P(("group", "exp"), ("seq", "tp"), None),
        check_vma=False,
    )
```

```python
import functools
import math

import jax
import jax.numpy as jnp
from jax import lax
from jax.experimental import pallas as pl
from jax.experimental.pallas import tpu as pltpu
from jax.sharding import PartitionSpec as P

HEADS = 32
KV_HEADS = 8
HEAD_DIM = 128
PROMPT = 256
CAP = 16
LEAD = 3
SUM_CHUNKS = 4
ROW_CHUNKS = 4
ROW_LAG = 2
GUEST_LAG = 1
HOLD = 7
ATT_EARLY = 3
SPLIT = 2
FIRST_RELAYS = 1
END_CHUNKS = 2
KV_LAG = 2
SIB_LAG = 1
END_LEAD = 6
SUM_LAG = 3

epsilon = 1e-06
masked_score = -1e30
MESH = pl.DeviceIdType.MESH
F32 = jnp.float32
BF16 = jnp.bfloat16


def kernel(
    n, plen_ref, kv_hbm, routes_hbm, gates_hbm, gain_hbm, q_hbm, wg_hbm, wu_hbm, wd_hbm,
    out_ref,
    routes_ref, gates_ref, gain_ref, kv_raw, qbuf, wg, wu, wd, kvbuf, att, groutes, sel, xsel, xbuf, part, rbuf, fin, ret, acc,
    w_sem, kv_local, kv_send, kv_recv, q_send, q_recv, g_sem, x_send, xs_send, f_send, x_recv,
    a_send, a_recv, r_send, r_recv, y_send, y_recv,
):
    z = lax.axis_index("seq")
    c = lax.axis_index("tp")
    sib = 1 - c
    has_left = z > 0
    has_right = z < n - 1
    end = (z == 0) | (z == n - 1)
    inner = (z > 0) & (z < n - 1)
    hosts = (z == 1) | (z == n - 2)
    guest = jnp.where(z == 1, 0, n - 1)
    host = jnp.where(z == 0, 1, n - 2)
    end_heads = END_CHUNKS * KV_HEADS // ROW_CHUNKS

    def go_left(h):
        return (z > 1) | ((z == 1) & (h < end_heads))

    def go_right(h):
        return (z < n - 2) | ((z == n - 2) & (h < end_heads))

    left, right, other = {"seq": z - 1}, {"seq": z + 1}, {"tp": sib}
    tokens = qbuf.shape[1]
    piece = kv_hbm.shape[0]
    groups = HEADS // KV_HEADS
    span = groups * HEAD_DIM
    width = att.shape[2]
    two = 2
    lag = KV_LAG * (n - 3) + SIB_LAG

    barrier = pltpu.get_barrier_semaphore()

    @pl.when(has_left)
    def _():
        for e in range(two):
            pl.semaphore_signal(barrier, inc=1, device_id={"seq": z - 1, "tp": e}, device_id_type=MESH)

    @pl.when(has_right)
    def _():
        for e in range(two):
            pl.semaphore_signal(barrier, inc=1, device_id={"seq": z + 1, "tp": e}, device_id_type=MESH)

    pl.semaphore_signal(barrier, inc=1, device_id=other, device_id_type=MESH)

    loads = [
        pltpu.make_async_copy(q_hbm, qbuf.at[0], w_sem.at[0]),
        pltpu.make_async_copy(wg_hbm, wg, w_sem.at[1]),
        pltpu.make_async_copy(wu_hbm, wu, w_sem.at[2]),
        pltpu.make_async_copy(wd_hbm, wd, w_sem.at[3]),
    ]
    own_kv = pltpu.make_async_copy(kv_hbm, kv_raw, kv_local.at[0])
    small = [
        pltpu.make_async_copy(routes_hbm, routes_ref, w_sem.at[4]),
        pltpu.make_async_copy(gates_hbm, gates_ref, w_sem.at[5]),
        pltpu.make_async_copy(gain_hbm, gain_ref, w_sem.at[6]),
    ]
    own_kv.start()
    for copy in small:
        copy.start()
    loads[0].start()

    own_kv.wait()
    block = 16 if piece % 16 == 0 else 8
    lines = 2 * KV_HEADS
    row = lax.broadcasted_iota(jnp.int32, (block * lines, block * lines), 0)
    column = lax.broadcasted_iota(jnp.int32, (block * lines, block * lines), 1)
    turn = (column == (row % block) * lines + row // block).astype(BF16)
    for b in range(piece // block):
        rows = kv_raw[b * block:(b + 1) * block].reshape(block * lines, HEAD_DIM)
        turned = jnp.dot(turn, rows, preferred_element_type=F32).astype(BF16)
        for i in range(lines):
            kvbuf[i // 2, i % 2, z, c, b * block:(b + 1) * block] = turned[i * block:(i + 1) * block]
    for copy in small:
        copy.wait()
    loads[0].wait()

    tri = (
        lax.broadcasted_iota(jnp.int32, (tokens, tokens), 0)
        <= lax.broadcasted_iota(jnp.int32, (tokens, tokens), 1)
    ).astype(F32)
    slots = lax.broadcasted_iota(jnp.int32, (CAP, tokens), 0).astype(F32)

    def picks(routes):
        chosen = []
        for e in range(two):
            hit = jnp.max((routes == e).astype(F32), axis=0, keepdims=True)
            rank = jnp.dot(jnp.broadcast_to(hit, (CAP, tokens)), tri, preferred_element_type=F32)
            chosen.append(jnp.where((rank - 1.0 == slots) & (hit > 0.0), 1.0, 0.0))
        return jnp.concatenate(chosen, axis=0)

    sel[0] = picks(routes_ref[...]).astype(BF16)

    pl.semaphore_wait(barrier, 1 + 2 * has_left.astype(jnp.int32) + 2 * has_right.astype(jnp.int32))

    def remote(src, dst, send, recv, device):
        return pltpu.make_async_remote_copy(
            src_ref=src, dst_ref=dst, send_sem=send, recv_sem=recv,
            device_id=device, device_id_type=MESH,
        )

    def kv_copy(h, oz, oc, way, device):
        slot = kvbuf.at[h, :, oz, oc]
        return remote(slot, slot, kv_send.at[h, oz, way], kv_recv.at[h, oz, oc], device)

    def pass_kv(h, oz, way):
        if way != 1:
            @pl.when(go_left(h))
            def _():
                kv_copy(h, oz, c, 0, left).start()

        if way != 0:
            @pl.when(go_right(h))
            def _():
                kv_copy(h, oz, c, 1, right).start()

        @pl.when(inner | (h < end_heads))
        def _():
            kv_copy(h, oz, c, 2, other).start()

    def query_copy(h):
        cols = pl.ds(pl.multiple_of(h * span, span), span)
        return remote(
            qbuf.at[0, :, cols], qbuf.at[1, :, cols], q_send.at[h], q_recv.at[h], {"seq": host}
        )

    def route_copy():
        return remote(routes_ref, groutes, g_sem.at[0], g_sem.at[1], {"seq": host})

    @pl.when(end)
    def _():
        route_copy().start()

    @pl.when(inner)
    def _():
        for h in range(LEAD):
            pass_kv(h, z, 2)

    @pl.when(end)
    def _():
        for h in range(END_LEAD):
            pass_kv(h, z, 2)
        for h in range(min(END_LEAD, end_heads), KV_HEADS):
            if h >= end_heads:
                query_copy(h).start()
            if h + END_LEAD - end_heads in range(END_LEAD, KV_HEADS):
                pass_kv(h + END_LEAD - end_heads, z, 2)

    for load in loads[1:]:
        load.start()

    @pl.when(hosts)
    def _():
        route_copy().wait_recv()
        sel[1] = picks(groutes[...]).astype(BF16)

    plen = plen_ref[0]
    keys = n * two * piece
    position = lax.broadcasted_iota(jnp.int32, (1, keys), 1)
    allowed = (position >= PROMPT) | (position < plen)

    def attend(h, s):
        base = pl.multiple_of(h * span, span)
        query = jnp.concatenate(
            [qbuf[s, :, pl.ds(base + g * HEAD_DIM, HEAD_DIM)] for g in range(groups)], axis=0
        )
        key_rows = kvbuf[h, 0].reshape(keys, HEAD_DIM)
        value_rows = kvbuf[h, 1].reshape(keys, HEAD_DIM)
        scores = lax.dot_general(
            query, key_rows, (((1,), (1,)), ((), ())), preferred_element_type=F32
        ) * (1.0 / math.sqrt(HEAD_DIM))
        scores = jnp.where(allowed, scores, masked_score)
        weights = jnp.exp(scores - jnp.max(scores, axis=1, keepdims=True))
        total = jnp.sum(weights, axis=1, keepdims=True)
        summed = jnp.dot(weights.astype(BF16), value_rows, preferred_element_type=F32)
        result = (summed / total).astype(BF16)
        for g in range(groups):
            att[s, :, pl.ds(base + g * HEAD_DIM, HEAD_DIM)] = result[g * tokens:(g + 1) * tokens]

    cut = width // ROW_CHUNKS
    per_cut = KV_HEADS // ROW_CHUNKS

    def columns(k):
        return pl.ds(pl.multiple_of(k * cut, cut), cut)

    def origin_of(s):
        return jnp.where(s == 0, z, guest)

    def row_copy(s, e, k, way):
        return remote(
            xsel.at[s, e, :, columns(k)], xbuf.at[origin_of(s), c, :, columns(k)],
            x_send.at[s, e, k, way], x_recv.at[origin_of(s), c, k],
            {"seq": z - 1 if way == 0 else z + 1, "tp": e},
        )

    def near_copy(s, k):
        return remote(
            xsel.at[s, sib, :, columns(k)], xbuf.at[origin_of(s), c, :, columns(k)],
            xs_send.at[s, k], x_recv.at[origin_of(s), c, k], other,
        )

    def far_copy(oz, oc, k, way):
        slot = xbuf.at[oz, oc, :, columns(k)]
        return remote(
            slot, slot, f_send.at[oz, oc, k], x_recv.at[oz, oc, k], left if way == 0 else right
        )

    def att_copy(k):
        return remote(
            att.at[1, :, columns(k)], att.at[0, :, columns(k)], a_send.at[k], a_recv.at[k],
            {"seq": guest},
        )

    def whole_rows(s, k):
        return k * per_cut + per_cut - 1 + lag + s * GUEST_LAG

    def start_rows(s, k, late):
        for way, edge in ((0, z == 1), (1, z == n - 2)):
            @pl.when(~edge if late else edge)
            def _():
                for e in range(two):
                    row_copy(s, e, k, way).start()

    def send_rows(r, s, k):
        picked = jnp.dot(sel[s], att[s, :, columns(k)], preferred_element_type=F32).astype(BF16)
        for e in range(two):
            xsel[s, e, :, columns(k)] = picked[e * CAP:(e + 1) * CAP]
        @pl.when((s == 1) & (r >= HOLD))
        def _():
            start_rows(s, k, True)

        @pl.when((s == 0) & inner)
        def _():
            start_rows(0, k, False)

        for way, far_end in ((0, z == n - 1), (1, z == 0)):
            @pl.when(far_end & (k < END_CHUNKS))
            def _():
                for e in range(two):
                    row_copy(0, e, k, way).start()

        @pl.when((s == 1) & (k < ATT_EARLY))
        def _():
            att_copy(k).start()

        near_copy(s, k).start()
        xbuf[origin_of(s), c, :, columns(k)] = xsel[s, c, :, columns(k)]

    def relay(oz, k, ok, way):
        @pl.when(ok)
        def _():
            for oc in range(two):
                far_copy(oz, oc, k, way).wait_recv()
                far_copy(oz, oc, k, way).start()

    def relay_round(r):
        def one(k, inner_carry):
            from_end = whole_rows(0, k) + KV_LAG + ROW_LAG
            sent = jnp.where(k < END_CHUNKS, from_end, jnp.maximum(whole_rows(1, k), HOLD))
            handed = (k < END_CHUNKS) & (r == from_end)
            relay(0, k, handed & (z == 1), 1)
            relay(n - 1, k, handed & (z == n - 2), 0)
            for d in range(1, n - 2):
                due = r == sent + ROW_LAG * d
                relay(0, k, due & (z - d == 1), 1)
                relay(n - 1, k, due & (z + d == n - 2), 0)
            return inner_carry

        lax.fori_loop(0, ROW_CHUNKS, one, 0)

    reach = jnp.where(end, end_heads, KV_HEADS)

    def kv_round(r, carry):
        @pl.when(inner & (r + LEAD < KV_HEADS))
        def _():
            pass_kv(r + LEAD, z, 2)

        for d in range(1, n):
            h = r - KV_LAG * (d - 1)
            live = (h >= 0) & (h < reach)

            @pl.when(live & (z - d >= 0))
            def _():
                kv_copy(h, z - d, c, 2, other).wait_recv()
                pass_kv(h, z - d, 1)

            @pl.when(live & (z + d < n))
            def _():
                kv_copy(h, z + d, c, 2, other).wait_recv()
                pass_kv(h, z + d, 0)

        @pl.when(r == HOLD)
        def _():
            for k in range(END_CHUNKS, ROW_CHUNKS):
                if whole_rows(1, k) < HOLD:
                    @pl.when(hosts)
                    def _():
                        start_rows(1, k, True)

        def one(s, inner_carry):
            h = r - lag - s * GUEST_LAG - KV_LAG * end.astype(jnp.int32)

            @pl.when((h >= s * end_heads) & (h < reach) & ((s == 0) | hosts))
            def _():
                @pl.when(s == 0)
                def _():
                    for oz in range(n):
                        kv_copy(h, oz, sib, 2, other).wait_recv()

                @pl.when(s == 1)
                def _():
                    query_copy(h).wait_recv()

                attend(h, s)

                @pl.when(h % per_cut == per_cut - 1)
                def _():
                    send_rows(r, s, h // per_cut)

            return inner_carry

        lax.fori_loop(0, two, one, 0)
        relay_round(r)
        return carry

    attend_rounds = max(KV_HEADS + lag + GUEST_LAG, HOLD + 1)
    relay_rounds = attend_rounds + ROW_LAG * (n - 3)

    lax.fori_loop(0, attend_rounds, kv_round, 0)

    @pl.when(inner)
    def _():
        def own_rows(k, carry):
            start_rows(0, k, True)
            return carry

        lax.fori_loop(0, ROW_CHUNKS, own_rows, 0)

    def drain_kv(h, carry):
        for oz in range(n):
            @pl.when(go_left(h) & (oz >= z))
            def _():
                kv_copy(h, oz, c, 0, left).wait_send()

            @pl.when(go_right(h) & (oz <= z))
            def _():
                kv_copy(h, oz, c, 1, right).wait_send()

            @pl.when(inner | (h < end_heads))
            def _():
                kv_copy(h, oz, c, 2, other).wait_send()

        @pl.when(end & (h >= end_heads))
        def _():
            query_copy(h).wait_send()

        return carry

    @pl.when(end)
    def _():
        lax.fori_loop(0, KV_HEADS, drain_kv, 0)
        route_copy().wait_send()

    for load in loads[1:]:
        load.wait()

    rows_here = two * CAP
    strip = width // SUM_CHUNKS
    pairs = n // two

    def sum_copy(way, dest, k, device):
        return remote(
            part.at[dest, k], rbuf.at[way, dest, k], r_send.at[way, dest, k], r_recv.at[way, dest, k],
            device,
        )

    def gather_rows(oz, k):
        here = (oz == z) | (hosts & (oz == guest))

        @pl.when(end & ~here)
        def _():
            for oc in range(two):
                far_copy(oz, oc, k, 0).wait_recv()

        @pl.when((oz == z) | (here & (k >= END_CHUNKS)))
        def _():
            far_copy(oz, sib, k, 0).wait_recv()

    def send_sum(dest, k):
        @pl.when(z == 0)
        def _():
            sum_copy(0, dest, k, right).start()

        @pl.when(z == n - 1)
        def _():
            sum_copy(1, dest, k, left).start()

    def expert(first, count, sends):
        squares, gate_part, up_part = 0.0, 0.0, 0.0
        for k in range(ROW_CHUNKS):
            for i in range(count):
                gather_rows(first + i, k)
            here = slice(k * cut, (k + 1) * cut)
            rows = xbuf[pl.ds(first, count), :, :, here].reshape(count * rows_here, cut).astype(F32)
            squares += jnp.sum(rows * rows, axis=1, keepdims=True)
            gained = (rows * gain_ref[:, here]).astype(BF16)
            gate_part += jnp.dot(gained, wg[here], preferred_element_type=F32)
            up_part += jnp.dot(gained, wu[here], preferred_element_type=F32)
        scale = lax.rsqrt(squares / width + epsilon)
        gate_part *= scale
        up_part *= scale
        hidden = (gate_part / (1.0 + jnp.exp(-gate_part)) * up_part).astype(BF16)
        for k in range(SUM_CHUNKS):
            done = jnp.dot(
                hidden, wd[:, k * strip:(k + 1) * strip], preferred_element_type=F32
            ).astype(BF16)
            for i in range(count):
                part[first + i, k] = done[i * rows_here:(i + 1) * rows_here]

            @pl.when(k < sends)
            def _():
                send_sum(first, k)

    near = z // two

    @pl.when(hosts)
    def _():
        expert(near * two, two, 0)

    def own_relays(d, start, stop):
        def one(k, carry):
            relay(z - d, k, z - d >= 1, 1)
            relay(z + d, k, z + d <= n - 2, 0)
            return carry

        lax.fori_loop(start, stop, one, 0)

    early = FIRST_RELAYS if n == 4 else ROW_CHUNKS
    begin = jnp.where(hosts, two, 0)

    def far_step(j, carry):
        p = lax.rem(near + j // two, pairs)
        i = j % two
        oz = p * two + jnp.where(p == pairs - 1, 1 - i, i)
        closing = end & (j == n)

        @pl.when(inner & (j == begin))
        def _():
            def later(r, inner_carry):
                relay_round(r)
                return inner_carry

            lax.fori_loop(attend_rounds, relay_rounds, later, 0)
            for d in range(1, n - 2):
                own_relays(d, 0, early)

        @pl.when(inner & (j == begin + 1))
        def _():
            for d in range(1, n - 2):
                own_relays(d, early, ROW_CHUNKS)

            @pl.when(hosts)
            def _():
                for k in range(max(ATT_EARLY, END_CHUNKS), ROW_CHUNKS):
                    att_copy(k).start()

        oz = jnp.where(closing, z, jnp.where(end & (j == 0), host, oz))

        @pl.when(inner & (j == begin + 1))
        def _():
            lax.fori_loop(0, KV_HEADS, drain_kv, 0)

        @pl.when(closing)
        def _():
            for k in range(SPLIT, SUM_CHUNKS):
                send_sum(host, k)
            for k in range(END_CHUNKS, ROW_CHUNKS):
                att_copy(k).wait_recv()
                send_rows(0, 0, k)

        @pl.when(closing | ((j < n) & jnp.where(hosts, j >= two, jnp.where(end, j != 1, True))))
        def _():
            sends = jnp.where(j == 0, SPLIT, jnp.where(end & (j < n), SUM_CHUNKS, 0))
            expert(oz, 1, sends)

        return carry

    lax.fori_loop(0, n + 1, far_step, 0)

    routes = routes_ref[...]
    gates = gates_ref[...]
    select = picks(routes)
    combine = []
    for e in range(two):
        gate = jnp.sum(jnp.where(routes == e, gates, 0.0), axis=0, keepdims=True)
        combine.append(select[e * CAP:(e + 1) * CAP] * gate)
    cw = jnp.transpose(jnp.concatenate(combine, axis=0))
    first = cw.astype(BF16)
    rest = cw - first.astype(F32)
    second = rest.astype(BF16)
    third = (rest - second.astype(F32)).astype(BF16)
    def pass_sum(way, dest, k, joins, device):
        @pl.when(joins)
        def _():
            sum_copy(way, dest, k, device).wait_recv()
            part[dest, k] = (part[dest, k].astype(F32) + rbuf[way, dest, k].astype(F32)).astype(BF16)

        sum_copy(way, dest, k, device).start()

    def sum_round(t, carry):
        i = t - SUM_LAG * z
        dest = n - 1 - i // SUM_CHUNKS

        @pl.when(inner & (i >= 0) & (dest > z))
        def _():
            pass_sum(0, dest, i % SUM_CHUNKS, has_left, right)

        i_back = t - SUM_LAG * (n - 1 - z)
        home = i_back // SUM_CHUNKS

        @pl.when(inner & (i_back >= 0) & (home < z))
        def _():
            pass_sum(1, home, i_back % SUM_CHUNKS, has_right, left)

        return carry

    sum_rounds = max(SUM_CHUNKS * (n - 2) + SUM_LAG, SUM_CHUNKS + SUM_LAG * (n - 2))
    lax.fori_loop(0, sum_rounds, sum_round, 0)

    @pl.when(hosts)
    def _():
        for k in range(END_CHUNKS, ROW_CHUNKS):
            att_copy(k).wait_send()

    def drain_rows(k, carry):
        for s in range(two):
            for way, edge, mine in ((0, z == 1, z == n - 1), (1, z == n - 2, z == 0)):
                to_host = mine & (k < END_CHUNKS)

                @pl.when(inner | to_host if s == 0 else hosts & ~edge & (k >= END_CHUNKS))
                def _():
                    for e in range(two):
                        row_copy(s, e, k, way).wait_send()

            @pl.when((s == 0) | (hosts & (k >= END_CHUNKS)))
            def _():
                near_copy(s, k).wait_send()

        for oz in range(n):
            from_left = (oz < z) & ~((oz == 0) & (z == 1))
            from_right = (oz > z) & ~((oz == n - 1) & (z == n - 2))

            handed = hosts & (oz == guest) & (k < END_CHUNKS)

            @pl.when(inner & (from_left | from_right | handed))
            def _():
                for oc in range(two):
                    far_copy(oz, oc, k, 0).wait_send()

        return carry

    lax.fori_loop(0, ROW_CHUNKS, drain_rows, 0)

    def result_copy(oc, k):
        cols = pl.ds(k * strip, strip)
        return remote(fin.at[sib, :, cols], ret.at[oc, :, cols], y_send.at[k], y_recv.at[k], other)

    for k in range(SUM_CHUNKS):
        cols = slice(k * strip, (k + 1) * strip)
        acc[...] = part[z, k].astype(F32)

        @pl.when(has_left)
        def _():
            sum_copy(0, z, k, right).wait_recv()
            acc[...] += rbuf[0, z, k].astype(F32)

        @pl.when(has_right)
        def _():
            sum_copy(1, z, k, left).wait_recv()
            acc[...] += rbuf[1, z, k].astype(F32)

        fin[:, :, cols] = acc[...].astype(BF16).reshape(two, CAP, strip)
        result_copy(c, k).start()
        ret[c, :, cols] = fin[c, :, cols]

    for k in range(SUM_CHUNKS):
        cols = slice(k * strip, (k + 1) * strip)
        result_copy(sib, k).wait_recv()
        returned = ret[:, :, cols].reshape(rows_here, strip)
        total = (
            jnp.dot(first, returned, preferred_element_type=F32)
            + jnp.dot(second, returned, preferred_element_type=F32)
            + jnp.dot(third, returned, preferred_element_type=F32)
        )
        out_ref[:, cols] = (att[0, :, cols].astype(F32) + total).astype(BF16)

    for k in range(SUM_CHUNKS):
        result_copy(c, k).wait_send()

    for oz in range(n):
        for k in range(SUM_CHUNKS):
            @pl.when(oz > z)
            def _():
                sum_copy(0, oz, k, right).wait_send()

            @pl.when(oz < z)
            def _():
                sum_copy(1, oz, k, left).wait_send()


def body(
    queries, keys_values, prompt_lengths, routes, gate_weights, norm_gain, w_gate, w_up, w_down
):
    n = lax.axis_size("seq")
    tokens, width = queries.shape[1:]
    piece = keys_values.shape[1]
    ff = w_gate.shape[2]
    kv = keys_values[0].reshape(piece, 2, KV_HEADS, HEAD_DIM).transpose(0, 2, 1, 3)
    kv = kv.reshape(piece, 2 * KV_HEADS, HEAD_DIM)
    top = routes.shape[2]
    strip = width // SUM_CHUNKS
    vmem = pl.BlockSpec(memory_space=pltpu.VMEM)
    hbm = pl.BlockSpec(memory_space=pltpu.HBM)
    dma = pltpu.SemaphoreType.DMA
    mixed = pl.pallas_call(
        functools.partial(kernel, n),
        out_shape=jax.ShapeDtypeStruct((tokens, width), BF16),
        in_specs=[pl.BlockSpec(memory_space=pltpu.SMEM)] + [hbm] * 8,
        out_specs=vmem,
        scratch_shapes=[
            pltpu.VMEM((top, tokens), jnp.int32),
            pltpu.VMEM((top, tokens), F32),
            pltpu.VMEM((1, width), F32),
            pltpu.VMEM((piece, 2 * KV_HEADS, HEAD_DIM), BF16),
            pltpu.VMEM((2, tokens, width), BF16),
            pltpu.VMEM((width, ff), BF16),
            pltpu.VMEM((width, ff), BF16),
            pltpu.VMEM((ff, width), BF16),
            pltpu.VMEM((KV_HEADS, 2, n, 2, piece, HEAD_DIM), BF16),
            pltpu.VMEM((2, tokens, width), BF16),
            pltpu.VMEM((top, tokens), jnp.int32),
            pltpu.VMEM((2, 2 * CAP, tokens), BF16),
            pltpu.VMEM((2, 2, CAP, width), BF16),
            pltpu.VMEM((n, 2, CAP, width), BF16),
            pltpu.VMEM((n, SUM_CHUNKS, 2 * CAP, strip), BF16),
            pltpu.VMEM((2, n, SUM_CHUNKS, 2 * CAP, strip), BF16),
            pltpu.VMEM((2, CAP, width), BF16),
            pltpu.VMEM((2, CAP, width), BF16),
            pltpu.VMEM((2 * CAP, strip), F32),
            dma((7,)),
            dma((1,)),
            dma((KV_HEADS, n, 3)),
            dma((KV_HEADS, n, 2)),
            dma((KV_HEADS,)),
            dma((KV_HEADS,)),
            dma((2,)),
            dma((2, 2, ROW_CHUNKS, 2)),
            dma((2, ROW_CHUNKS)),
            dma((n, 2, ROW_CHUNKS)),
            dma((n, 2, ROW_CHUNKS)),
            dma((ROW_CHUNKS,)),
            dma((ROW_CHUNKS,)),
            dma((2, n, SUM_CHUNKS)),
            dma((2, n, SUM_CHUNKS)),
            dma((SUM_CHUNKS,)),
            dma((SUM_CHUNKS,)),
        ],
        compiler_params=pltpu.CompilerParams(
            collective_id=0, has_side_effects=True, vmem_limit_bytes=60 * 1024 * 1024
        ),
    )(
        prompt_lengths, kv, routes[0].T, gate_weights[0].T, norm_gain[None], queries[0],
        w_gate[0], w_up[0], w_down[0],
    )
    return mixed[None]


def solution(mesh):
    return jax.shard_map(
        body,
        mesh=mesh,
        in_specs=(
            P(("group", "exp"), ("seq", "tp"), None),
            P(("group", "exp"), ("seq", "tp"), None, None),
            P(("group", "exp")),
            P(("group", "exp"), ("seq", "tp"), None),
            P(("group", "exp"), ("seq", "tp"), None),
            P(),
            P("tp", None, "seq"),
            P("tp", None, "seq"),
            P("tp", "seq", None),
        ),
        out_specs=P(("group", "exp"), ("seq", "tp"), None),
        check_vma=False,
    )
```
